32 devices in a mesh: groups: 2 (over x), long: 16 (over z, y, core).
Axes of the slice: x: 2, y: 2, z: 4, core: 2. Of those that a mesh axis runs over, the one named last changes fastest.
Arguments:
- initial_state: float32 [2, 8192, 128], P(None, ('groups', 'long')), parts along dimension 1, may hold values from -6 to 6
- adjoint_state: float32 [2, 8192, 128], P(None, ('groups', 'long')), parts along dimension 1, may hold values from -6 to 6
- current_gates: float32 [8, 2, 128, 128], P('groups'), parts along dimension 0, may hold values from -0.375 to 0.375
Outputs:
- final_state: float32 [2, 8192, 128], P(None, ('groups', 'long')), parts along dimension 1
- final_adjoint: float32 [2, 8192, 128], P(None, ('groups', 'long')), parts along dimension 1
The draws below stay inside these ranges and needn't reach their ends.
There are 2 independent parts, one for each index of `groups`. The reference program is written for one: setup_inputs(seed, part) draws one part's arguments, and reference() takes and returns one part's arrays. A program takes and returns all parts, laid end to end along the dimension named above; each array names one. Nothing has to cross between parts.
All inputs are finite; a program needn't handle non-finite values.
Results may differ from the reference program's by a relative error of at most 0.00017.
Values sent between devices are 32-bit elements; how exact they have to be, the bound alone decides.
A program may use at most 64 MiB of HBM per device.

```python
import jax
import jax.numpy as jnp
from jax import lax

GATE = 128
SECTIONS = 4
NS_ITERS = 8
AMP_ROWS = 4096
N_LONG = 16


def level_of(own_key, extent, pieces, least, high):
    loudness, own = 1.0, jax.random.fold_in(own_key, 6)
    for position, blocks in pieces:
        draws = jnp.exp(jax.random.uniform(jax.random.fold_in(own, position), (blocks,), jnp.float32, least / len(pieces), high / len(pieces)))
        loudness = loudness * jnp.repeat(draws, extent[position] // blocks).reshape([-1 if axis == position else 1 for axis in range(len(extent))])
    return loudness


def bell_draw(key, shape, spread, bound, pieces=(), dtype=jnp.bfloat16):
    values = spread * jax.random.normal(key, shape, jnp.float32)
    if pieces:
        values = values * level_of(key, shape, pieces, -0.22, 0.18)
    return jnp.clip(values, -bound, bound).astype(dtype)


def setup_inputs(seed: int = 0, part: int = 0) -> dict:
    seeds = jax.random.split(jax.random.key(seed), 4)
    part_keys = jax.random.split(jax.random.fold_in(seeds[3], part), 4)
    initial_state = bell_draw(part_keys[0], (2, AMP_ROWS, GATE), 1.0, 6.0, ((1, 16),), jnp.float32)
    adjoint_state = bell_draw(part_keys[1], (2, AMP_ROWS, GATE), 1.0, 6.0, ((1, 16),), jnp.float32)
    current_gates = bell_draw(part_keys[2], (SECTIONS, 2, GATE, GATE), (2 * GATE) ** -0.5, 0.375, (), jnp.float32)
    return {"initial_state": initial_state, "adjoint_state": adjoint_state, "current_gates": current_gates}


HIGHEST = lax.Precision.HIGHEST

def einsum_high(pattern, left_side, right_side):
    return jnp.einsum(pattern, left_side, right_side, precision=HIGHEST, preferred_element_type=jnp.float32)

def matmul_high(left_side, right_side):
    return jnp.dot(left_side, right_side, precision=HIGHEST, preferred_element_type=jnp.float32)

def rows_product(left_side, right_side):
    return lax.dot_general(left_side, right_side, (((0,), (0,)), ((), ())), precision=HIGHEST, preferred_element_type=jnp.float32)

def polar_factor(summed_real, summed_imag, sweeps):
    norm_scale = lax.rsqrt(jnp.sum(summed_real * summed_real + summed_imag * summed_imag) + 1e-06)
    iterate_real = summed_real * norm_scale
    iterate_imag = summed_imag * norm_scale
    for sweep_index in range(sweeps):
        gram_real = rows_product(iterate_real, iterate_real) + rows_product(iterate_imag, iterate_imag)
        gram_imag = rows_product(iterate_real, iterate_imag) - rows_product(iterate_imag, iterate_real)
        product_real = matmul_high(iterate_real, gram_real) - matmul_high(iterate_imag, gram_imag)
        product_imag = matmul_high(iterate_real, gram_imag) + matmul_high(iterate_imag, gram_real)
        iterate_real = 1.5 * iterate_real - 0.5 * product_real
        iterate_imag = 1.5 * iterate_imag - 0.5 * product_imag
    return (iterate_real, iterate_imag)

def split_view(amplitudes, partner_bit):
    outer_count = N_LONG // 2 ** (partner_bit + 1)
    inner_count = amplitudes.shape[1] // (2 * outer_count)
    lane_half = amplitudes.shape[2] // 2
    return amplitudes.reshape(amplitudes.shape[0], outer_count, 2, inner_count, 2, lane_half)

def apply_gate(gate_real, gate_imag, viewed):
    lane_half = gate_real.shape[0] // 2
    blocks_real = gate_real.reshape(2, lane_half, 2, lane_half)
    blocks_imag = gate_imag.reshape(2, lane_half, 2, lane_half)
    pattern = 'acbd,hbmed->hamec'
    out_real = einsum_high(pattern, blocks_real, viewed[0]) - einsum_high(pattern, blocks_imag, viewed[1])
    out_imag = einsum_high(pattern, blocks_real, viewed[1]) + einsum_high(pattern, blocks_imag, viewed[0])
    return jnp.stack([out_real, out_imag])

def environment(adjoint_view, state_view):
    pattern = 'hamec,hbmed->acbd'
    summed_real = einsum_high(pattern, adjoint_view[0], state_view[0]) + einsum_high(pattern, adjoint_view[1], state_view[1])
    summed_imag = einsum_high(pattern, adjoint_view[1], state_view[0]) - einsum_high(pattern, adjoint_view[0], state_view[1])
    gate_width = summed_real.shape[0] * summed_real.shape[1]
    return (summed_real.reshape(gate_width, gate_width), summed_imag.reshape(gate_width, gate_width))

def reference(initial_state, adjoint_state, current_gates):
    bit_count = N_LONG.bit_length() - 1
    partner_bits = [bit_count - 1, bit_count // 2, 0, 1]
    state_now = initial_state
    adjoint_now = adjoint_state
    for section_index in range(SECTIONS):
        partner_bit = partner_bits[section_index % 4]
        state_view = split_view(state_now, partner_bit)
        adjoint_view = apply_gate(current_gates[section_index, 0], current_gates[section_index, 1], split_view(adjoint_now, partner_bit))
        summed_real, summed_imag = environment(adjoint_view, state_view)
        gate_real, gate_imag = polar_factor(summed_real, summed_imag, NS_ITERS)
        state_view = apply_gate(gate_real, gate_imag, state_view)
        state_now = state_view.reshape(initial_state.shape)
        adjoint_now = adjoint_view.reshape(adjoint_state.shape)
    return (state_now, adjoint_now)
```

```python
import functools

import jax
import jax.numpy as jnp
from jax import lax
from jax.experimental import pallas as pl
from jax.experimental.pallas import tpu as pltpu
from jax.sharding import PartitionSpec as P

SECTIONS = 4
NS_ITERS = 8
MESH = pl.DeviceIdType.MESH
ADJ_IN, PSI_IN, ADJ_OUT, PSI_OUT, RS, AG, CROSS, MID = 0, 1, 2, 3, 4, 8, 12, 14
PHASES = 14
CHAINED = ()
BACK = ((2, 3), (0,), (1,), ())


def split(x):
    high = x.astype(jnp.bfloat16)
    return high, (x - high.astype(jnp.float32)).astype(jnp.bfloat16)


def dot3(left, right, contract):
    def dot(a, b):
        return lax.dot_general(
            a, b, (contract, ((), ())), preferred_element_type=jnp.float32
        )

    return dot(left[0], right[0]) + (dot(left[0], right[1]) + dot(left[1], right[0]))


def embed_out(real, imag):
    return jnp.concatenate(
        [
            jnp.concatenate([real, -imag], axis=1),
            jnp.concatenate([imag, real], axis=1),
        ],
        axis=0,
    )


def swap_plane(plane, q, per):
    rows, lanes = plane.shape
    stride = per << q
    rolled = pltpu.roll(plane, lanes // 2, 1)
    low = lax.broadcasted_iota(jnp.int32, (stride, lanes), 1) < lanes // 2
    blocks = []
    for start in range(0, rows, 2 * stride):
        mid, end = start + stride, start + 2 * stride
        blocks.append(jnp.where(low, plane[start:mid], rolled[mid:end]))
        blocks.append(jnp.where(low, rolled[start:mid], plane[mid:end]))
    return jnp.concatenate(blocks, axis=0)


def halves(x, q, per):
    stride = per << q
    starts = range(0, x.shape[0], 2 * stride)
    return [
        jnp.concatenate([x[k + bit * stride : k + (bit + 1) * stride] for k in starts], axis=0)
        for bit in range(2)
    ]


def swap(x, q, per):
    lanes = x.shape[1] // 2
    return jnp.concatenate(
        [swap_plane(x[:, :lanes], q, per), swap_plane(x[:, lanes:], q, per)], axis=1
    )


def embed(v):
    gate = v.shape[0]
    real, imag = v[:, :gate], v[:, gate:]
    return jnp.concatenate([v, jnp.concatenate([-imag, real], axis=1)], axis=0)


def contract_cross(cross, fitted):
    rows, gate = cross[0].shape
    half = gate // 2
    left = jnp.concatenate(
        [
            jnp.concatenate([cross[4 * u + 2 * v + plane] for u in range(2) for plane in range(2)], axis=1)
            for v in range(2)
        ],
        axis=0,
    )
    full = tuple(embed(x) for x in split(fitted))
    right = tuple(
        jnp.concatenate(
            [
                jnp.concatenate([x[u * half : (u + 1) * half], x[gate + u * half : gate + (u + 1) * half]], axis=0)
                for u in range(2)
            ],
            axis=1,
        )
        for x in full
    )
    out = dot3(split(left), right, ((1,), (1,)))
    low, high = out[:rows], out[rows:]
    return (
        jnp.concatenate([low[:, :half], high[:, :half]], axis=1),
        jnp.concatenate([low[:, half:], high[:, half:]], axis=1),
    )


def polar(x, sweeps):
    gate = x.shape[0]
    norm = lax.rsqrt(jnp.sum(x * x, keepdims=True) + 1e-06)

    def sweep(_, a):
        high, low = split(a)

        full = (embed(high), embed(low))
        def product(left, axis):
            def dot(u, v):
                return lax.dot_general(
                    u, v, (((1,), (axis,)), ((), ())), preferred_element_type=jnp.float32
                )

            both = dot(jnp.concatenate(left, axis=0), full[0])
            return both[:gate] + (both[gate:] + dot(left[0], full[1]))

        gram = product((high, low), 1)
        return 1.5 * a - 0.5 * product(split(gram), 0)

    return lax.fori_loop(0, sweeps, sweep, x * norm, unroll=8)


def kernel(
    used, order, extra_bits,
    psi_in, adj_in, gates_in, psi_out, adj_out,
    psi_buf, adj_buf, gates, phi_t, phi_cross, psi_send, adj_send,
    part, rs_buf, cross, cross_buf, ag_buf, mid_buf, mid_cross,
    send_sem, recv_sem, mid_send, mid_recv, local_sem,
):
    group = lax.axis_index("groups")
    me = lax.axis_index("long")
    n = 2 ** len(used)
    extra = 2 ** len(extra_bits)
    rows = psi_in.shape[1]
    gate = psi_in.shape[2]
    owners = n // 2
    first = n // 4
    own = gate // owners
    per = rows // owners

    def gather(value, bits):
        out = 0
        for k, bit in enumerate(bits):
            out = out + lax.rem(lax.div(value, 2**bit), 2) * 2**k
        return out

    def scatter(value, bits):
        out = 0
        for k, bit in enumerate(bits):
            out = out + lax.rem(lax.div(value, 2**k), 2) * 2**bit
        return out

    slot = gather(me, used)
    layer = gather(me, extra_bits)

    def peer(j):
        return scatter(j, used) + scatter(layer, extra_bits)

    def layer_peer(j):
        return scatter(slot, used) + scatter(j, extra_bits)

    def others(fn, mine=slot, count=n):
        def step(off, carry):
            fn(lax.rem(mine + off, count))
            return carry

        lax.fori_loop(1, count, step, 0)

    quarter = n // 4
    column = lax.div(slot, quarter)
    upper = lax.div(column, 2)
    inner = column + upper * (3 - 2 * column)

    def far_first(fn, ranks=(0, 1, 2, 3)):
        for rank in ranks:
            place = (3, 2, 1 - inner, inner)[rank]
            base = (place + upper * (3 - 2 * place)) * quarter

            def step(k, carry):
                fn(base + lax.rem(slot + 1 + k, quarter))
                return carry

            lax.fori_loop(0, quarter - (rank == 3), step, 0)

    def owners_far_first(fn, among=False):
        for rank in range(2):
            base = (2 - rank + upper * (2 * rank - 1)) * quarter

            def step(k, carry):
                fn(base + lax.rem(slot + 1 + k, quarter))
                return carry

            lax.fori_loop(0, quarter - rank, step, 0)

            if rank == 1 and not among:

                @pl.when(jnp.logical_not(is_owner))
                def _():
                    fn(base + lax.rem(slot, quarter))

    is_owner = inner == 1

    def remote(src, dst, phase, target):
        return pltpu.make_async_remote_copy(
            src_ref=src,
            dst_ref=dst,
            send_sem=send_sem.at[phase],
            recv_sem=recv_sem.at[phase],
            device_id={"groups": group, "long": target},
            device_id_type=MESH,
        )

    def block(ref, j, size):
        return ref.at[:, pl.ds(pl.multiple_of(j * size, size), size), :]

    def arrived(ref, phase):
        remote(ref, ref, phase, peer(lax.rem(slot + 1, n))).wait_recv()

    def departed(ref, phase):
        remote(ref, ref, phase, peer(lax.rem(slot + 1, n))).wait_send()

    index = slot - first

    def signal(j, target):
        pl.semaphore_signal(
            barrier, inc=1, device_id={"groups": group, "long": target(j)}, device_id_type=MESH
        )

    barrier = pltpu.get_barrier_semaphore()

    @pl.when(is_owner)
    def _():
        far_first(lambda j: signal(j, peer))
        if extra > 1:
            others(lambda j: signal(j, layer_peer), layer, extra)
        pl.semaphore_wait(barrier, n + extra - 2)

    @pl.when(jnp.logical_not(is_owner))
    def _():
        owners_far_first(lambda j: signal(j, peer))
        pl.semaphore_wait(barrier, owners)

    def inward(src, dst, phase):
        return lambda j: remote(block(src, j - first, per), block(dst, slot, per), phase, peer(j)).start()

    def outward(src, dst, phase):
        return lambda j: remote(block(src, j, per), block(dst, index, per), phase, peer(j)).start()

    owners_far_first(inward(adj_in, adj_buf, ADJ_IN))
    owners_far_first(inward(psi_in, psi_buf, PSI_IN))

    def joined(ref):
        return jnp.concatenate([ref[0], ref[1]], axis=1)

    def put(ref, x):
        for q in order[::-1]:
            x = swap(x, q, per)
        ref[0] = x[:, :gate]
        ref[1] = x[:, gate:]

    def advance_adjoint(phi, s):
        full = split(embed_out(gates[s, 0], gates[s, 1]))
        phi = dot3(split(phi), full, ((1,), (1,)))
        if s in CHAINED:
            for u, rows_u in enumerate(halves(phi, order[s], per)):
                high, low = split(rows_u.T)
                phi_cross[CHAINED.index(s), u, 0] = high
                phi_cross[CHAINED.index(s), u, 1] = low
        else:
            high, low = split(phi.T)
            phi_t[s, 0] = high
            phi_t[s, 1] = low
        return phi

    def outer(left, right):
        both = dot3(left, right, ((1,), (0,)))
        return both[:gate, :gate] + both[gate:, gate:], both[gate:, :gate] - both[:gate, gate:]

    def own_copy(src, dst, phase):
        return pltpu.make_async_copy(src, dst, recv_sem.at[phase])

    @pl.when(is_owner)
    def _():
        gate_copy = pltpu.make_async_copy(gates_in, gates, local_sem.at[0])
        gate_copy.start()
        own_copy(block(adj_in, index, per), block(adj_buf, slot, per), ADJ_IN).start()
        own_copy(block(psi_in, index, per), block(psi_buf, slot, per), PSI_IN).start()
        mine = pl.ds(pl.multiple_of(index * own, own), own)

        gate_copy.wait()
        arrived(adj_buf, ADJ_IN)
        phi = joined(adj_buf)
        for s in range(SECTIONS):
            phi = advance_adjoint(swap(phi, order[s], per), s)
        put(adj_send, phi)
        own_copy(block(adj_send, slot, per), block(adj_out, index, per), ADJ_OUT).start()
        adj_back = outward(adj_send, adj_out, ADJ_OUT)
        arrived(psi_buf, PSI_IN)
        psi = swap(joined(psi_buf), order[0], per)
        fitted = None

        def among(fn):
            owners_far_first(fn, True)

        def over_layers(buf, total, kind):
            buf[layer] = total

            def across(j, here):
                return pltpu.make_async_remote_copy(
                    src_ref=buf.at[here],
                    dst_ref=buf.at[here],
                    send_sem=mid_send.at[kind, j],
                    recv_sem=mid_recv.at[kind, here],
                    device_id={"groups": group, "long": layer_peer(j)},
                    device_id_type=MESH,
                )

            others(lambda j: across(j, layer).start(), layer, extra)
            others(lambda j: across(j, j).wait_recv(), layer, extra)
            others(lambda j: across(j, layer).wait_send(), layer, extra)
            total = buf[0]
            for j in range(1, extra):
                total = total + buf[j]
            return total

        def reduced(src, buf, phase):
            arrived(buf.at[pl.ds(0, owners - 1)], phase)
            buf[index] = src[:, mine, :]
            total = buf[0]
            for j in range(1, owners):
                total = total + buf[j]
            return total

        def send_cross(k, u):
            planes = pl.ds(4 * u, 4)
            among(
                lambda j: remote(
                    block(cross.at[k, planes], j - first, own), cross_buf.at[k, index, planes], CROSS + k, peer(j)
                ).start()
            )

        for s in range(SECTIONS):
            ahead = CHAINED.index(s + 1) if s + 1 in CHAINED else None
            state = split(psi)
            if s in CHAINED:
                k = CHAINED.index(s)
                total = reduced(cross.at[k], cross_buf.at[k], CROSS + k)
                if extra > 1:
                    total = over_layers(mid_cross.at[k], total, SECTIONS + k)
                ag_buf[s, 0, mine, :], ag_buf[s, 1, mine, :] = contract_cross(total, fitted)
            else:
                part[s, 0], part[s, 1] = outer((phi_t[s, 0], phi_t[s, 1]), state)
                among(
                    lambda j: remote(block(part.at[s], j - first, own), rs_buf.at[s, index], RS + s, peer(j)).start()
                )
                if ahead is not None:
                    for u in range(2):
                        for v in range(2):
                            right = tuple(halves(x, order[s + 1], per)[v] for x in state)
                            cross[ahead, 4 * u + 2 * v], cross[ahead, 4 * u + 2 * v + 1] = outer(
                                (phi_cross[ahead, u, 0], phi_cross[ahead, u, 1]), right
                            )
                        if u == 0:
                            send_cross(ahead, u)
                total = reduced(part.at[s], rs_buf.at[s], RS + s)
                if extra > 1:
                    total = over_layers(mid_buf.at[s], total, s)
                ag_buf[s, :, mine, :] = total
            held = block(ag_buf.at[s], index, own)
            among(lambda j: remote(held, held, AG + s, peer(j)).start())
            if s not in CHAINED and ahead is not None:
                send_cross(ahead, 1)
            if s in CHAINED:
                full = split(embed_out(fitted[:, :gate], fitted[:, gate:]))
                psi = swap(dot3(split(psi), full, ((1,), (1,))), order[s], per)
            for rank in BACK[s]:
                far_first(adj_back, (rank,))
            arrived(block(ag_buf.at[s], 0, (owners - 1) * own), AG + s)
            fitted = polar(jnp.concatenate([ag_buf[s, 0], ag_buf[s, 1]], axis=1), NS_ITERS)
            if ahead is None:
                full = split(embed_out(fitted[:, :gate], fitted[:, gate:]))
                psi = dot3(split(psi), full, ((1,), (1,)))
                if s + 1 < SECTIONS:
                    psi = swap(psi, order[s + 1], per)

        put(psi_send, psi)
        far_first(outward(psi_send, psi_out, PSI_OUT))
        own_copy(block(psi_send, slot, per), block(psi_out, index, per), PSI_OUT).start()
        for s in range(SECTIONS):
            sent = block(part.at[s], 0, (owners - 1) * own)
            departed(sent, AG + s)
            if s in CHAINED:
                k = CHAINED.index(s)
                departed(block(cross.at[k], 0, (owners - 1) * own), CROSS + k)
            else:
                departed(sent, RS + s)
        departed(block(adj_in, 0, (owners - 1) * per), ADJ_IN)
        departed(block(psi_in, 0, (owners - 1) * per), PSI_IN)
        departed(block(adj_send, 0, (n - 1) * per), ADJ_OUT)
        departed(block(psi_send, 0, (n - 1) * per), PSI_OUT)

    @pl.when(jnp.logical_not(is_owner))
    def _():
        departed(adj_in, ADJ_IN)
        departed(psi_in, PSI_IN)

    arrived(adj_out, ADJ_OUT)
    arrived(psi_out, PSI_OUT)


def shards(initial_state, adjoint_state, current_gates):
    bit_count = lax.axis_size("long").bit_length() - 1
    partner_bits = [bit_count - 1, bit_count // 2, 0, 1]
    used = sorted(set(partner_bits))
    assert len(used) == SECTIONS
    order = [used.index(bit) for bit in partner_bits]
    extra_bits = [bit for bit in range(bit_count) if bit not in used]
    n, extra = 2 ** len(used), 2 ** len(extra_bits)
    planes, rows, gate = initial_state.shape
    owners = n // 2
    own = gate // owners
    held = n * (rows // owners)
    f32, bf16 = jnp.float32, jnp.bfloat16
    anywhere = pl.BlockSpec(memory_space=pl.ANY)
    return tuple(
        pl.pallas_call(
            functools.partial(kernel, used, order, extra_bits),
            out_shape=[pltpu.VMEM(initial_state.shape, f32)] * 2,
            in_specs=[anywhere] * 3,
            out_specs=[pl.BlockSpec(memory_space=pltpu.VMEM)] * 2,
            scratch_shapes=[
                pltpu.VMEM((2, held, gate), f32),
                pltpu.VMEM((2, held, gate), f32),
                pltpu.VMEM(current_gates.shape, f32),
                pltpu.VMEM((SECTIONS, 2, 2 * gate, held), bf16),
                pltpu.VMEM((2, 2, 2, 2 * gate, held // 2), bf16),
                pltpu.VMEM((2, held, gate), f32),
                pltpu.VMEM((2, held, gate), f32),
                pltpu.VMEM((SECTIONS, 2, gate, gate), f32),
                pltpu.VMEM((SECTIONS, owners, 2, own, gate), f32),
                pltpu.VMEM((2, 8, gate, gate), f32),
                pltpu.VMEM((2, owners, 8, own, gate), f32),
                pltpu.VMEM((SECTIONS, 2, gate, gate), f32),
                pltpu.VMEM((SECTIONS, extra, 2, own, gate), f32),
                pltpu.VMEM((2, extra, 8, own, gate), f32),
                pltpu.SemaphoreType.DMA((PHASES,)),
                pltpu.SemaphoreType.DMA((PHASES,)),
                pltpu.SemaphoreType.DMA((SECTIONS + 2 if extra > 1 else 1, extra)),
                pltpu.SemaphoreType.DMA((SECTIONS + 2 if extra > 1 else 1, extra)),
                pltpu.SemaphoreType.DMA((1,)),
            ],
            compiler_params=pltpu.CompilerParams(collective_id=0, has_side_effects=True),
            name="sweep",
        )(initial_state, adjoint_state, current_gates)
    )


def solution(mesh):
    return jax.shard_map(
        shards,
        mesh=mesh,
        in_specs=(
            P(None, ("groups", "long"), None),
            P(None, ("groups", "long"), None),
            P("groups", None, None, None),
        ),
        out_specs=(P(None, ("groups", "long"), None), P(None, ("groups", "long"), None)),
        check_vma=False,
    )
```

```python
import functools

import jax
import jax.numpy as jnp
from jax import lax
from jax.experimental import pallas as pl
from jax.experimental.pallas import tpu as pltpu
from jax.sharding import PartitionSpec as P

SECTIONS = 4
NS_ITERS = 8
MESH = pl.DeviceIdType.MESH
ADJ_IN, PSI_IN, ADJ_OUT, PSI_OUT, RS, AG, CROSS, MID = 0, 1, 2, 3, 4, 8, 12, 14
PHASES = 14
CHAINED = (1, 3)
BACK = ((), (0, 1, 2, 3), (), ())


def split(x):
    high = x.astype(jnp.bfloat16)
    return high, (x - high.astype(jnp.float32)).astype(jnp.bfloat16)


def dot3(left, right, contract):
    def dot(a, b):
        return lax.dot_general(
            a, b, (contract, ((), ())), preferred_element_type=jnp.float32
        )

    return dot(left[0], right[0]) + (dot(left[0], right[1]) + dot(left[1], right[0]))


def embed_out(real, imag):
    return jnp.concatenate(
        [
            jnp.concatenate([real, -imag], axis=1),
            jnp.concatenate([imag, real], axis=1),
        ],
        axis=0,
    )


def swap_plane(plane, q, per):
    rows, lanes = plane.shape
    stride = per << q
    rolled = pltpu.roll(plane, lanes // 2, 1)
    low = lax.broadcasted_iota(jnp.int32, (stride, lanes), 1) < lanes // 2
    blocks = []
    for start in range(0, rows, 2 * stride):
        mid, end = start + stride, start + 2 * stride
        blocks.append(jnp.where(low, plane[start:mid], rolled[mid:end]))
        blocks.append(jnp.where(low, rolled[start:mid], plane[mid:end]))
    return jnp.concatenate(blocks, axis=0)


def halves(x, q, per):
    stride = per << q
    starts = range(0, x.shape[0], 2 * stride)
    return [
        jnp.concatenate([x[k + bit * stride : k + (bit + 1) * stride] for k in starts], axis=0)
        for bit in range(2)
    ]


def swap(x, q, per):
    lanes = x.shape[1] // 2
    return jnp.concatenate(
        [swap_plane(x[:, :lanes], q, per), swap_plane(x[:, lanes:], q, per)], axis=1
    )


def embed(v):
    gate = v.shape[0]
    real, imag = v[:, :gate], v[:, gate:]
    return jnp.concatenate([v, jnp.concatenate([-imag, real], axis=1)], axis=0)


def contract_cross(cross, fitted):
    rows, gate = cross[0].shape
    half = gate // 2
    left = jnp.concatenate(
        [
            jnp.concatenate([cross[4 * u + 2 * v + plane] for u in range(2) for plane in range(2)], axis=1)
            for v in range(2)
        ],
        axis=0,
    )
    full = tuple(embed(x) for x in split(fitted))
    right = tuple(
        jnp.concatenate(
            [
                jnp.concatenate([x[u * half : (u + 1) * half], x[gate + u * half : gate + (u + 1) * half]], axis=0)
                for u in range(2)
            ],
            axis=1,
        )
        for x in full
    )
    out = dot3(split(left), right, ((1,), (1,)))
    low, high = out[:rows], out[rows:]
    return (
        jnp.concatenate([low[:, :half], high[:, :half]], axis=1),
        jnp.concatenate([low[:, half:], high[:, half:]], axis=1),
    )


def polar(x, sweeps):
    gate = x.shape[0]
    norm = lax.rsqrt(jnp.sum(x * x, keepdims=True) + 1e-06)

    def sweep(_, a):
        high, low = split(a)

        full = (embed(high), embed(low))
        def product(left, axis):
            def dot(u, v):
                return lax.dot_general(
                    u, v, (((1,), (axis,)), ((), ())), preferred_element_type=jnp.float32
                )

            both = dot(jnp.concatenate(left, axis=0), full[0])
            return both[:gate] + (both[gate:] + dot(left[0], full[1]))

        gram = product((high, low), 1)
        return 1.5 * a - 0.5 * product(split(gram), 0)

    return lax.fori_loop(0, sweeps, sweep, x * norm, unroll=8)


def kernel(
    used, order, extra_bits,
    psi_in, adj_in, gates_in, psi_out, adj_out,
    psi_buf, adj_buf, gates, phi_t, phi_cross, psi_send, adj_send,
    part, rs_buf, cross, cross_buf, ag_buf, mid_buf, mid_cross,
    send_sem, recv_sem, mid_send, mid_recv, local_sem,
):
    group = lax.axis_index("groups")
    me = lax.axis_index("long")
    n = 2 ** len(used)
    extra = 2 ** len(extra_bits)
    rows = psi_in.shape[1]
    gate = psi_in.shape[2]
    owners = n // 2
    first = n // 4
    own = gate // owners
    per = rows // owners

    def gather(value, bits):
        out = 0
        for k, bit in enumerate(bits):
            out = out + lax.rem(lax.div(value, 2**bit), 2) * 2**k
        return out

    def scatter(value, bits):
        out = 0
        for k, bit in enumerate(bits):
            out = out + lax.rem(lax.div(value, 2**k), 2) * 2**bit
        return out

    slot = gather(me, used)
    layer = gather(me, extra_bits)

    def peer(j):
        return scatter(j, used) + scatter(layer, extra_bits)

    def layer_peer(j):
        return scatter(slot, used) + scatter(j, extra_bits)

    def others(fn, mine=slot, count=n):
        def step(off, carry):
            fn(lax.rem(mine + off, count))
            return carry

        lax.fori_loop(1, count, step, 0)

    quarter = n // 4
    column = lax.div(slot, quarter)
    upper = lax.div(column, 2)
    inner = column + upper * (3 - 2 * column)

    def far_first(fn, ranks=(0, 1, 2, 3)):
        for rank in ranks:
            place = (3, 2, 1 - inner, inner)[rank]
            base = (place + upper * (3 - 2 * place)) * quarter

            def step(k, carry):
                fn(base + lax.rem(slot + 1 + k, quarter))
                return carry

            lax.fori_loop(0, quarter - (rank == 3), step, 0)

    def owners_far_first(fn, among=False):
        for rank in range(2):
            base = (2 - rank + upper * (2 * rank - 1)) * quarter

            def step(k, carry):
                fn(base + lax.rem(slot + 1 + k, quarter))
                return carry

            lax.fori_loop(0, quarter - rank, step, 0)

            if rank == 1 and not among:

                @pl.when(jnp.logical_not(is_owner))
                def _():
                    fn(base + lax.rem(slot, quarter))

    is_owner = inner == 1

    def remote(src, dst, phase, target):
        return pltpu.make_async_remote_copy(
            src_ref=src,
            dst_ref=dst,
            send_sem=send_sem.at[phase],
            recv_sem=recv_sem.at[phase],
            device_id={"groups": group, "long": target},
            device_id_type=MESH,
        )

    def block(ref, j, size):
        return ref.at[:, pl.ds(pl.multiple_of(j * size, size), size), :]

    def arrived(ref, phase):
        remote(ref, ref, phase, peer(lax.rem(slot + 1, n))).wait_recv()

    def departed(ref, phase):
        remote(ref, ref, phase, peer(lax.rem(slot + 1, n))).wait_send()

    index = slot - first

    def signal(j, target):
        pl.semaphore_signal(
            barrier, inc=1, device_id={"groups": group, "long": target(j)}, device_id_type=MESH
        )

    barrier = pltpu.get_barrier_semaphore()

    @pl.when(is_owner)
    def _():
        far_first(lambda j: signal(j, peer))
        if extra > 1:
            others(lambda j: signal(j, layer_peer), layer, extra)
        pl.semaphore_wait(barrier, n + extra - 2)

    @pl.when(jnp.logical_not(is_owner))
    def _():
        owners_far_first(lambda j: signal(j, peer))
        pl.semaphore_wait(barrier, owners)

    def inward(src, dst, phase):
        return lambda j: remote(block(src, j - first, per), block(dst, slot, per), phase, peer(j)).start()

    def outward(src, dst, phase):
        return lambda j: remote(block(src, j, per), block(dst, index, per), phase, peer(j)).start()

    owners_far_first(inward(adj_in, adj_buf, ADJ_IN))
    owners_far_first(inward(psi_in, psi_buf, PSI_IN))

    def joined(ref):
        return jnp.concatenate([ref[0], ref[1]], axis=1)

    def put(ref, x):
        for q in order[::-1]:
            x = swap(x, q, per)
        ref[0] = x[:, :gate]
        ref[1] = x[:, gate:]

    def advance_adjoint(phi, s):
        full = split(embed_out(gates[s, 0], gates[s, 1]))
        phi = dot3(split(phi), full, ((1,), (1,)))
        if s in CHAINED:
            for u, rows_u in enumerate(halves(phi, order[s], per)):
                high, low = split(rows_u.T)
                phi_cross[CHAINED.index(s), u, 0] = high
                phi_cross[CHAINED.index(s), u, 1] = low
        else:
            high, low = split(phi.T)
            phi_t[s, 0] = high
            phi_t[s, 1] = low
        return phi

    def outer(left, right):
        both = dot3(left, right, ((1,), (0,)))
        return both[:gate, :gate] + both[gate:, gate:], both[gate:, :gate] - both[:gate, gate:]

    def own_copy(src, dst, phase):
        return pltpu.make_async_copy(src, dst, recv_sem.at[phase])

    @pl.when(is_owner)
    def _():
        gate_copy = pltpu.make_async_copy(gates_in, gates, local_sem.at[0])
        gate_copy.start()
        own_copy(block(adj_in, index, per), block(adj_buf, slot, per), ADJ_IN).start()
        own_copy(block(psi_in, index, per), block(psi_buf, slot, per), PSI_IN).start()
        mine = pl.ds(pl.multiple_of(index * own, own), own)

        gate_copy.wait()
        arrived(adj_buf, ADJ_IN)
        phi = joined(adj_buf)
        for s in range(SECTIONS):
            phi = advance_adjoint(swap(phi, order[s], per), s)
        put(adj_send, phi)
        own_copy(block(adj_send, slot, per), block(adj_out, index, per), ADJ_OUT).start()
        adj_back = outward(adj_send, adj_out, ADJ_OUT)
        arrived(psi_buf, PSI_IN)
        psi = swap(joined(psi_buf), order[0], per)
        fitted = None

        def among(fn):
            owners_far_first(fn, True)

        def over_layers(buf, total, kind):
            buf[layer] = total

            def across(j, here):
                return pltpu.make_async_remote_copy(
                    src_ref=buf.at[here],
                    dst_ref=buf.at[here],
                    send_sem=mid_send.at[kind, j],
                    recv_sem=mid_recv.at[kind, here],
                    device_id={"groups": group, "long": layer_peer(j)},
                    device_id_type=MESH,
                )

            others(lambda j: across(j, layer).start(), layer, extra)
            others(lambda j: across(j, j).wait_recv(), layer, extra)
            others(lambda j: across(j, layer).wait_send(), layer, extra)
            total = buf[0]
            for j in range(1, extra):
                total = total + buf[j]
            return total

        def reduced(src, buf, phase):
            arrived(buf.at[pl.ds(0, owners - 1)], phase)
            buf[index] = src[:, mine, :]
            total = buf[0]
            for j in range(1, owners):
                total = total + buf[j]
            return total

        def send_cross(k, u):
            planes = pl.ds(4 * u, 4)
            among(
                lambda j: remote(
                    block(cross.at[k, planes], j - first, own), cross_buf.at[k, index, planes], CROSS + k, peer(j)
                ).start()
            )

        for s in range(SECTIONS):
            ahead = CHAINED.index(s + 1) if s + 1 in CHAINED else None
            state = split(psi)
            if s in CHAINED:
                k = CHAINED.index(s)
                total = reduced(cross.at[k], cross_buf.at[k], CROSS + k)
                if extra > 1:
                    total = over_layers(mid_cross.at[k], total, SECTIONS + k)
                ag_buf[s, 0, mine, :], ag_buf[s, 1, mine, :] = contract_cross(total, fitted)
            else:
                part[s, 0], part[s, 1] = outer((phi_t[s, 0], phi_t[s, 1]), state)
                among(
                    lambda j: remote(block(part.at[s], j - first, own), rs_buf.at[s, index], RS + s, peer(j)).start()
                )
                if ahead is not None:
                    for u in range(2):
                        for v in range(2):
                            right = tuple(halves(x, order[s + 1], per)[v] for x in state)
                            cross[ahead, 4 * u + 2 * v], cross[ahead, 4 * u + 2 * v + 1] = outer(
                                (phi_cross[ahead, u, 0], phi_cross[ahead, u, 1]), right
                            )
                        if u == 0:
                            send_cross(ahead, u)
                total = reduced(part.at[s], rs_buf.at[s], RS + s)
                if extra > 1:
                    total = over_layers(mid_buf.at[s], total, s)
                ag_buf[s, :, mine, :] = total
            held = block(ag_buf.at[s], index, own)
            among(lambda j: remote(held, held, AG + s, peer(j)).start())
            if s not in CHAINED and ahead is not None:
                send_cross(ahead, 1)
            if s in CHAINED:
                full = split(embed_out(fitted[:, :gate], fitted[:, gate:]))
                psi = swap(dot3(split(psi), full, ((1,), (1,))), order[s], per)
            for rank in BACK[s]:
                far_first(adj_back, (rank,))
            arrived(block(ag_buf.at[s], 0, (owners - 1) * own), AG + s)
            fitted = polar(jnp.concatenate([ag_buf[s, 0], ag_buf[s, 1]], axis=1), NS_ITERS)
            if ahead is None:
                full = split(embed_out(fitted[:, :gate], fitted[:, gate:]))
                psi = dot3(split(psi), full, ((1,), (1,)))
                if s + 1 < SECTIONS:
                    psi = swap(psi, order[s + 1], per)

        put(psi_send, psi)
        far_first(outward(psi_send, psi_out, PSI_OUT))
        own_copy(block(psi_send, slot, per), block(psi_out, index, per), PSI_OUT).start()
        for s in range(SECTIONS):
            sent = block(part.at[s], 0, (owners - 1) * own)
            departed(sent, AG + s)
            if s in CHAINED:
                k = CHAINED.index(s)
                departed(block(cross.at[k], 0, (owners - 1) * own), CROSS + k)
            else:
                departed(sent, RS + s)
        departed(block(adj_in, 0, (owners - 1) * per), ADJ_IN)
        departed(block(psi_in, 0, (owners - 1) * per), PSI_IN)
        departed(block(adj_send, 0, (n - 1) * per), ADJ_OUT)
        departed(block(psi_send, 0, (n - 1) * per), PSI_OUT)

    @pl.when(jnp.logical_not(is_owner))
    def _():
        departed(adj_in, ADJ_IN)
        departed(psi_in, PSI_IN)

    arrived(adj_out, ADJ_OUT)
    arrived(psi_out, PSI_OUT)


def shards(initial_state, adjoint_state, current_gates):
    bit_count = lax.axis_size("long").bit_length() - 1
    partner_bits = [bit_count - 1, bit_count // 2, 0, 1]
    used = sorted(set(partner_bits))
    assert len(used) == SECTIONS
    order = [used.index(bit) for bit in partner_bits]
    extra_bits = [bit for bit in range(bit_count) if bit not in used]
    n, extra = 2 ** len(used), 2 ** len(extra_bits)
    planes, rows, gate = initial_state.shape
    owners = n // 2
    own = gate // owners
    held = n * (rows // owners)
    f32, bf16 = jnp.float32, jnp.bfloat16
    anywhere = pl.BlockSpec(memory_space=pl.ANY)
    return tuple(
        pl.pallas_call(
            functools.partial(kernel, used, order, extra_bits),
            out_shape=[pltpu.VMEM(initial_state.shape, f32)] * 2,
            in_specs=[anywhere] * 3,
            out_specs=[pl.BlockSpec(memory_space=pltpu.VMEM)] * 2,
            scratch_shapes=[
                pltpu.VMEM((2, held, gate), f32),
                pltpu.VMEM((2, held, gate), f32),
                pltpu.VMEM(current_gates.shape, f32),
                pltpu.VMEM((SECTIONS, 2, 2 * gate, held), bf16),
                pltpu.VMEM((2, 2, 2, 2 * gate, held // 2), bf16),
                pltpu.VMEM((2, held, gate), f32),
                pltpu.VMEM((2, held, gate), f32),
                pltpu.VMEM((SECTIONS, 2, gate, gate), f32),
                pltpu.VMEM((SECTIONS, owners, 2, own, gate), f32),
                pltpu.VMEM((2, 8, gate, gate), f32),
                pltpu.VMEM((2, owners, 8, own, gate), f32),
                pltpu.VMEM((SECTIONS, 2, gate, gate), f32),
                pltpu.VMEM((SECTIONS, extra, 2, own, gate), f32),
                pltpu.VMEM((2, extra, 8, own, gate), f32),
                pltpu.SemaphoreType.DMA((PHASES,)),
                pltpu.SemaphoreType.DMA((PHASES,)),
                pltpu.SemaphoreType.DMA((SECTIONS + 2 if extra > 1 else 1, extra)),
                pltpu.SemaphoreType.DMA((SECTIONS + 2 if extra > 1 else 1, extra)),
                pltpu.SemaphoreType.DMA((1,)),
            ],
            compiler_params=pltpu.CompilerParams(collective_id=0, has_side_effects=True),
            name="sweep",
        )(initial_state, adjoint_state, current_gates)
    )


def solution(mesh):
    return jax.shard_map(
        shards,
        mesh=mesh,
        in_specs=(
            P(None, ("groups", "long"), None),
            P(None, ("groups", "long"), None),
            P("groups", None, None, None),
        ),
        out_specs=(P(None, ("groups", "long"), None), P(None, ("groups", "long"), None)),
        check_vma=False,
    )
```

```python
import functools

import jax
import jax.numpy as jnp
from jax import lax
from jax.experimental import pallas as pl
from jax.experimental.pallas import tpu as pltpu
from jax.sharding import PartitionSpec as P

SECTIONS = 4
NS_ITERS = 8
MESH = pl.DeviceIdType.MESH
ADJ_IN, PSI_IN, ADJ_OUT, FAR, NEAR, HALF, FINAL, RS, AG, CROSS = 0, 1, 2, 3, 4, 5, 7, 11, 15, 19
CHAINED = (1, 3)
CORE = CROSS + len(CHAINED)
PHASES = CORE + 2 * len(CHAINED)
BACK = ((), (0, 1, 2, 3), (), (), ())
SEND = (((), ()), ((), ()), ((2, 3), (0, 1)), ((), ()))


def split(x):
    high = x.astype(jnp.bfloat16)
    return high, (x - high.astype(jnp.float32)).astype(jnp.bfloat16)


def dot3(left, right, contract):
    def dot(a, b):
        return lax.dot_general(
            a, b, (contract, ((), ())), preferred_element_type=jnp.float32
        )

    return dot(left[0], right[0]) + (dot(left[0], right[1]) + dot(left[1], right[0]))


def embed_out(real, imag):
    return jnp.concatenate(
        [
            jnp.concatenate([real, -imag], axis=1),
            jnp.concatenate([imag, real], axis=1),
        ],
        axis=0,
    )


def swap_plane(plane, stride):
    rows, lanes = plane.shape
    rolled = pltpu.roll(plane, lanes // 2, 1)
    low = lax.broadcasted_iota(jnp.int32, (stride, lanes), 1) < lanes // 2
    blocks = []
    for start in range(0, rows, 2 * stride):
        mid, end = start + stride, start + 2 * stride
        blocks.append(jnp.where(low, plane[start:mid], rolled[mid:end]))
        blocks.append(jnp.where(low, rolled[start:mid], plane[mid:end]))
    return jnp.concatenate(blocks, axis=0)


def halves(x, q, per):
    stride = per << q
    starts = range(0, x.shape[0], 2 * stride)
    return [
        jnp.concatenate([x[k + bit * stride : k + (bit + 1) * stride] for k in starts], axis=0)
        for bit in range(2)
    ]


def swap_rows(x, stride):
    lanes = x.shape[1] // 2
    return jnp.concatenate(
        [swap_plane(x[:, :lanes], stride), swap_plane(x[:, lanes:], stride)], axis=1
    )


def swap(x, q, per):
    return swap_rows(x, per << q)


def embed(v):
    gate = v.shape[0]
    real, imag = v[:, :gate], v[:, gate:]
    return jnp.concatenate([v, jnp.concatenate([-imag, real], axis=1)], axis=0)


def contract_cross(cross, fitted):
    rows, gate = cross[0].shape
    half = gate // 2
    left = jnp.concatenate(
        [
            jnp.concatenate([cross[4 * u + 2 * v + plane] for u in range(2) for plane in range(2)], axis=1)
            for v in range(2)
        ],
        axis=0,
    )
    full = tuple(embed(x) for x in split(fitted))
    right = tuple(
        jnp.concatenate(
            [
                jnp.concatenate([x[u * half : (u + 1) * half], x[gate + u * half : gate + (u + 1) * half]], axis=0)
                for u in range(2)
            ],
            axis=1,
        )
        for x in full
    )
    out = dot3(split(left), right, ((1,), (1,)))
    low, high = out[:rows], out[rows:]
    return (
        jnp.concatenate([low[:, :half], high[:, :half]], axis=1),
        jnp.concatenate([low[:, half:], high[:, half:]], axis=1),
    )


def polar(x, sweeps):
    gate = x.shape[0]
    norm = lax.rsqrt(jnp.sum(x * x, keepdims=True) + 1e-06)

    def sweep(_, a):
        high, low = split(a)

        full = (embed(high), embed(low))
        def product(left, axis):
            def dot(u, v):
                return lax.dot_general(
                    u, v, (((1,), (axis,)), ((), ())), preferred_element_type=jnp.float32
                )

            both = dot(jnp.concatenate(left, axis=0), full[0])
            return both[:gate] + (both[gate:] + dot(left[0], full[1]))

        gram = product((high, low), 1)
        return 1.5 * a - 0.5 * product(split(gram), 0)

    return lax.fori_loop(0, sweeps, sweep, x * norm, unroll=8)


def kernel(
    used, order, extra_bits,
    psi_in, adj_in, gates_in, psi_out, adj_out,
    psi_buf, adj_buf, gates, phi_t, phi_cross, psi_send, adj_send,
    part, rs_buf, cross, pair_buf, chip_buf, cross_buf, ag_buf, final, half_gate, mid_buf, mid_cross,
    send_sem, recv_sem, mid_send, mid_recv, local_sem,
):
    group = lax.axis_index("groups")
    me = lax.axis_index("long")
    n = 2 ** len(used)
    extra = 2 ** len(extra_bits)
    rows = psi_in.shape[1]
    gate = psi_in.shape[2]
    owners = n // 2
    first = n // 4
    own = gate // owners
    per = rows // owners

    def gather(value, bits):
        out = 0
        for k, bit in enumerate(bits):
            out = out + lax.rem(lax.div(value, 2**bit), 2) * 2**k
        return out

    def scatter(value, bits):
        out = 0
        for k, bit in enumerate(bits):
            out = out + lax.rem(lax.div(value, 2**k), 2) * 2**bit
        return out

    slot = gather(me, used) if extra_bits else me
    layer = gather(me, extra_bits)

    def peer(j):
        return scatter(j, used) + scatter(layer, extra_bits) if extra_bits else j

    def layer_peer(j):
        return scatter(slot, used) + scatter(j, extra_bits)

    def others(fn, mine=slot, count=n):
        def step(off, carry):
            fn(lax.rem(mine + off, count))
            return carry

        lax.fori_loop(1, count, step, 0)

    quarter = n // 4
    column = lax.div(slot, quarter)
    upper = lax.div(column, 2)
    inner = column + upper * (3 - 2 * column)

    def far_first(fn, ranks=(0, 1, 2, 3)):
        for rank in ranks:
            place = (3, 2, 1 - inner, inner)[rank]
            base = (place + upper * (3 - 2 * place)) * quarter

            def step(k, carry):
                fn(base + lax.rem(slot + 1 + k, quarter))
                return carry

            for k in range(quarter - (rank == 3)):
                step(k, 0)

    def owners_far_first(fn, among=False):
        for rank in range(2):
            base = (2 - rank + upper * (2 * rank - 1)) * quarter

            def step(k, carry):
                fn(base + lax.rem(slot + 1 + k, quarter))
                return carry

            for k in range(quarter - rank):
                step(k, 0)

            if rank == 1 and not among:

                @pl.when(jnp.logical_not(is_owner))
                def _():
                    fn(base + lax.rem(slot, quarter))

    is_owner = inner == 1

    def remote(src, dst, phase, target):
        return pltpu.make_async_remote_copy(
            src_ref=src,
            dst_ref=dst,
            send_sem=send_sem.at[phase],
            recv_sem=recv_sem.at[phase],
            device_id={"groups": group, "long": target},
            device_id_type=MESH,
        )

    def block(ref, j, size):
        return ref.at[:, pl.ds(pl.multiple_of(j * size, size), size), :]

    def arrived(ref, phase):
        remote(ref, ref, phase, peer(lax.rem(slot + 1, n))).wait_recv()

    def departed(ref, phase):
        remote(ref, ref, phase, peer(lax.rem(slot + 1, n))).wait_send()

    index = slot - first

    def shard(k):
        return lax.rem(k, 2) * (owners // 2) + lax.div(k, 2)

    def signal(j, target):
        pl.semaphore_signal(
            barrier, inc=1, device_id={"groups": group, "long": target(j)}, device_id_type=MESH
        )

    barrier = pltpu.get_barrier_semaphore()

    @pl.when(is_owner)
    def _():
        far_first(lambda j: signal(j, peer))
        if extra > 1:
            others(lambda j: signal(j, layer_peer), layer, extra)
        pl.semaphore_wait(barrier, n + extra - 2)

    @pl.when(jnp.logical_not(is_owner))
    def _():
        owners_far_first(lambda j: signal(j, peer))
        pl.semaphore_wait(barrier, owners)

    def inward(src, dst, phase):
        return lambda j: remote(block(src, j - first, per), block(dst, slot, per), phase, peer(j)).start()

    def outward(src, dst, phase):
        return lambda j: remote(block(src, j, per), block(dst, index, per), phase, peer(j)).start()

    def bit_of(q):
        return lax.rem(lax.div(slot, 2**q), 2)

    def flipped(q):
        return peer(slot + (1 - 2 * bit_of(q)) * 2**q)

    def variant(near, far):
        return near + 2 * far

    near_bit, far_bit = bit_of(order[2]), bit_of(order[3])
    mine_at = variant(near_bit, far_bit)
    other_at = variant(near_bit, 1 - far_bit)
    chunks = owners // 2
    chips = owners // 2
    wide = gate // 2
    pair = rows // chunks

    def target_variant(j):
        return variant(lax.rem(lax.div(j, 2 ** order[2]), 2), lax.rem(lax.div(j, 2 ** order[3]), 2))

    def to_final(j):
        remote(
            block(psi_send, j, per),
            block(final.at[target_variant(j)], index, per),
            FINAL + lax.div(index, 2),
            peer(j),
        ).start()

    def pass_across():
        def step(k, carry):
            part_k = lax.rem(k + upper * (chunks // 2), chunks)
            ref = block(final.at[mine_at], part_k, pair)
            arrived(ref, FINAL + part_k)
            remote(ref, ref, FAR, flipped(order[3])).start()
            return carry

        lax.fori_loop(0, chunks, step, 0)
        remote(final.at[mine_at], final.at[mine_at], NEAR, flipped(order[2])).start()

    def gather_final():
        arrived(final.at[other_at], FAR)
        remote(final.at[other_at], final.at[other_at], NEAR, flipped(order[2])).start()
        arrived(final.at[pl.ds(0, 2)], NEAR)

    def keep_half(k, bit, x):
        half = gate // 2
        half_gate[k] = jnp.where(bit == 0, x[:half], x[half:])

    def fit(s):
        return polar(jnp.concatenate([ag_buf[s, 0], ag_buf[s, 1]], axis=1), NS_ITERS)

    def half_apply(x, k):
        full = embed_out(half_gate[k, :, :gate], half_gate[k, :, gate:])
        return dot3(split(x), split(full), ((1,), (1,)))

    def before_last():
        outs = []
        for far in range(2):
            both = [joined(final.at[variant(near, far)]) for near in range(2)]
            outs.append(half_apply(swap_rows(jnp.concatenate(both, axis=0), rows), 0))
        x = swap_plane(jnp.concatenate(outs, axis=0), 2 * rows)
        return jnp.concatenate([x[: 2 * rows], x[2 * rows :]], axis=1)

    def last(x):
        x = swap_plane(half_apply(x, 1), rows)
        psi_out[0] = x[:rows]
        psi_out[1] = x[rows:]

    def joined(ref):
        return jnp.concatenate([ref[0], ref[1]], axis=1)

    owners_far_first(inward(adj_in, adj_buf, ADJ_IN))
    owners_far_first(inward(psi_in, psi_buf, PSI_IN))

    def put(ref, x, done):
        for q in done[::-1]:
            x = swap(x, q, per)
        ref[0] = x[:, :gate]
        ref[1] = x[:, gate:]

    def advance_adjoint(phi, s):
        full = split(embed_out(gates[s, 0], gates[s, 1]))
        phi = dot3(split(phi), full, ((1,), (1,)))
        if s in CHAINED:
            for u, rows_u in enumerate(halves(phi, order[s], per)):
                high, low = split(rows_u.T)
                phi_cross[CHAINED.index(s), u, 0] = high
                phi_cross[CHAINED.index(s), u, 1] = low
        else:
            high, low = split(phi.T)
            phi_t[s, 0] = high
            phi_t[s, 1] = low
        return phi

    def outer(left, right):
        both = dot3(left, right, ((1,), (0,)))
        return both[:gate, :gate] + both[gate:, gate:], both[gate:, :gate] - both[:gate, gate:]

    def own_copy(src, dst, phase):
        return pltpu.make_async_copy(src, dst, recv_sem.at[phase])

    @pl.when(is_owner)
    def _():
        gate_copy = pltpu.make_async_copy(gates_in, gates, local_sem.at[0])
        gate_copy.start()
        own_copy(block(adj_in, index, per), block(adj_buf, slot, per), ADJ_IN).start()
        own_copy(block(psi_in, index, per), block(psi_buf, slot, per), PSI_IN).start()
        chip = lax.div(index, 2)
        parity = lax.rem(index, 2)
        mine = pl.ds(pl.multiple_of(shard(index) * own, own), own)

        gate_copy.wait()
        arrived(adj_buf, ADJ_IN)
        phi = joined(adj_buf)
        for s in range(SECTIONS):
            phi = advance_adjoint(swap(phi, order[s], per), s)
        put(adj_send, phi, order)
        own_copy(block(adj_send, slot, per), block(adj_out, index, per), ADJ_OUT).start()
        adj_back = outward(adj_send, adj_out, ADJ_OUT)
        for rank in BACK[SECTIONS]:
            far_first(adj_back, (rank,))
        arrived(psi_buf, PSI_IN)
        psi = swap(joined(psi_buf), order[0], per)
        fitted = None

        def among(fn):
            owners_far_first(fn, True)

        def over_layers(buf, total, kind):
            buf[layer] = total

            def across(j, here):
                return pltpu.make_async_remote_copy(
                    src_ref=buf.at[here],
                    dst_ref=buf.at[here],
                    send_sem=mid_send.at[kind, j],
                    recv_sem=mid_recv.at[kind, here],
                    device_id={"groups": group, "long": layer_peer(j)},
                    device_id_type=MESH,
                )

            others(lambda j: across(j, layer).start(), layer, extra)
            others(lambda j: across(j, j).wait_recv(), layer, extra)
            others(lambda j: across(j, layer).wait_send(), layer, extra)
            total = buf[0]
            for j in range(1, extra):
                total = total + buf[j]
            return total

        def reduced(src, buf, phase):
            arrived(buf.at[pl.ds(0, owners - 1)], phase)
            buf[index] = src[:, mine, :]
            total = buf[0]
            for j in range(1, owners):
                total = total + buf[j]
            return total

        def send_cross(k, u):
            planes = pl.ds(4 * u, 4)
            remote(
                block(cross.at[k, planes], 1 - parity, wide), pair_buf.at[k, planes], CORE + 2 * k + u, flipped(0)
            ).start()

        def pass_cross(k, u):
            planes = pl.ds(4 * u, 4)
            arrived(pair_buf.at[k, planes], CORE + 2 * k + u)
            rows_here = pl.ds(pl.multiple_of(parity * wide, wide), wide)
            chip_buf[k, planes] = cross[k, planes, rows_here, :] + pair_buf[k, planes]

            def step(off, carry):
                there = lax.rem(chip + off, chips)
                remote(
                    block(chip_buf.at[k, planes], there, own),
                    cross_buf.at[k, chip, planes],
                    CROSS + k,
                    peer(first + 2 * there + parity),
                ).start()
                return carry

            lax.fori_loop(1, chips, step, 0)

        def reduced_cross(k):
            arrived(cross_buf.at[k, pl.ds(0, chips - 1)], CROSS + k)
            cross_buf[k, chip] = chip_buf[k, :, pl.ds(pl.multiple_of(chip * own, own), own), :]
            total = cross_buf[k, 0]
            for j in range(1, chips):
                total = total + cross_buf[k, j]
            return total

        def send_plain(x):
            put(psi_send, x, order[:3])
            pltpu.make_async_copy(
                block(psi_send, slot, per), block(final.at[mine_at], index, per), recv_sem.at[FINAL + lax.div(index, 2)]
            ).start()

        def fill_cross(k, s, x):
            state = split(x)
            for u in range(2):
                for v in range(2):
                    right = tuple(halves(h, order[s + 1], per)[v] for h in state)
                    cross[k, 4 * u + 2 * v], cross[k, 4 * u + 2 * v + 1] = outer(
                        (phi_cross[k, u, 0], phi_cross[k, u, 1]), right
                    )
                send_cross(k, u)
            for u in range(2):
                pass_cross(k, u)

        def apply(x, gate_pair):
            return dot3(split(x), split(embed_out(gate_pair[:, :gate], gate_pair[:, gate:])), ((1,), (1,)))

        outer_peer = 3 * upper * quarter + lax.rem(slot, quarter)

        def share_half(k, bit, x):
            keep_half(k, bit, x)
            if k == 0:
                remote(half_gate.at[k], half_gate.at[k], HALF, peer(outer_peer)).start()

        for s in range(SECTIONS):
            ahead = CHAINED.index(s + 1) if s + 1 in CHAINED else None
            if s in CHAINED:
                k = CHAINED.index(s)
                total = reduced_cross(k)
                if extra > 1:
                    total = over_layers(mid_cross.at[k], total, SECTIONS + k)
                ag_buf[s, 0, mine, :], ag_buf[s, 1, mine, :] = contract_cross(total, fitted)
            else:
                part[s, 0], part[s, 1] = outer((phi_t[s, 0], phi_t[s, 1]), split(psi))
                among(
                    lambda j: remote(block(part.at[s], shard(j - first), own), rs_buf.at[s, index], RS + s, peer(j)).start()
                )
                if ahead is not None:
                    fill_cross(ahead, s, psi)
                if s == 2:
                    send_plain(psi)
                for rank in SEND[s][0]:
                    far_first(to_final, (rank,))
                total = reduced(part.at[s], rs_buf.at[s], RS + s)
                if extra > 1:
                    total = over_layers(mid_buf.at[s], total, s)
                ag_buf[s, :, mine, :] = total
            held = block(ag_buf.at[s], shard(index), own)
            among(lambda j: remote(held, held, AG + s, peer(j)).start())
            if s == SECTIONS - 1:
                far_first(lambda j: remote(held, held, AG + s, peer(j)).start(), (0, 2))
            if s in CHAINED and s < SECTIONS - 1:
                psi = swap(apply(psi, fitted), order[s], per)
                if ahead is not None:
                    fill_cross(ahead, s, psi)
                if s == 2:
                    send_plain(psi)
            for rank in BACK[s]:
                far_first(adj_back, (rank,))
            for rank in SEND[s][1]:
                far_first(to_final, (rank,))
            if s == SECTIONS - 1:
                pass_across()
            arrived(block(ag_buf.at[s], 0, (owners - 1) * own), AG + s)
            fitted = fit(s)
            if s == SECTIONS - 2:
                share_half(0, near_bit, fitted)
            if s == SECTIONS - 1:
                share_half(1, far_bit, fitted)
            if ahead is None and s < SECTIONS - 1:
                psi = swap(apply(psi, fitted), order[s + 1], per)

        gather_final()
        last(before_last())
        for s in range(SECTIONS):
            sent = block(part.at[s], 0, (owners - 1) * own)
            departed(block(psi_send, 0, (n - 1) * own) if s == SECTIONS - 1 else sent, AG + s)
            if s in CHAINED:
                k = CHAINED.index(s)
                departed(block(chip_buf.at[k], 0, (chips - 1) * own), CROSS + k)
                for u in range(2):
                    departed(pair_buf.at[k, pl.ds(4 * u, 4)], CORE + 2 * k + u)
            else:
                departed(sent, RS + s)
        departed(block(adj_in, 0, (owners - 1) * per), ADJ_IN)
        departed(block(psi_in, 0, (owners - 1) * per), PSI_IN)
        departed(block(adj_send, 0, (n - 1) * per), ADJ_OUT)
        departed(block(psi_send, 0, (n - 1) * per), FINAL + lax.div(index, 2))
        departed(half_gate.at[0], HALF)

    @pl.when(jnp.logical_not(is_owner))
    def _():
        pass_across()
        gather_final()
        arrived(half_gate.at[0], HALF)
        x = before_last()
        arrived(ag_buf.at[SECTIONS - 1], AG + SECTIONS - 1)
        keep_half(1, far_bit, fit(SECTIONS - 1))
        last(x)
        departed(adj_in, ADJ_IN)
        departed(psi_in, PSI_IN)

    departed(final.at[mine_at], FAR)
    departed(final.at[pl.ds(0, 2)], NEAR)
    arrived(adj_out, ADJ_OUT)


def shards(initial_state, adjoint_state, current_gates):
    bit_count = lax.axis_size("long").bit_length() - 1
    partner_bits = [bit_count - 1, bit_count // 2, 0, 1]
    used = sorted(set(partner_bits))
    assert len(used) == SECTIONS
    order = [used.index(bit) for bit in partner_bits]
    extra_bits = [bit for bit in range(bit_count) if bit not in used]
    n, extra = 2 ** len(used), 2 ** len(extra_bits)
    planes, rows, gate = initial_state.shape
    owners = n // 2
    own = gate // owners
    held = n * (rows // owners)
    f32, bf16 = jnp.float32, jnp.bfloat16
    anywhere = pl.BlockSpec(memory_space=pl.ANY)
    return tuple(
        pl.pallas_call(
            functools.partial(kernel, used, order, extra_bits),
            out_shape=[pltpu.VMEM(initial_state.shape, f32)] * 2,
            in_specs=[anywhere] * 3,
            out_specs=[pl.BlockSpec(memory_space=pltpu.VMEM)] * 2,
            scratch_shapes=[
                pltpu.VMEM((2, held, gate), f32),
                pltpu.VMEM((2, held, gate), f32),
                pltpu.VMEM(current_gates.shape, f32),
                pltpu.VMEM((SECTIONS, 2, 2 * gate, held), bf16),
                pltpu.VMEM((len(CHAINED), 2, 2, 2 * gate, held // 2), bf16),
                pltpu.VMEM((2, held, gate), f32),
                pltpu.VMEM((2, held, gate), f32),
                pltpu.VMEM((SECTIONS, 2, gate, gate), f32),
                pltpu.VMEM((SECTIONS, owners, 2, own, gate), f32),
                pltpu.VMEM((len(CHAINED), 8, gate, gate), f32),
                pltpu.VMEM((len(CHAINED), 8, gate // 2, gate), f32),
                pltpu.VMEM((len(CHAINED), 8, gate // 2, gate), f32),
                pltpu.VMEM((len(CHAINED), owners // 2, 8, own, gate), f32),
                pltpu.VMEM((SECTIONS, 2, gate, gate), f32),
                pltpu.VMEM((4, planes, rows, gate), f32),
                pltpu.VMEM((2, gate // 2, 2 * gate), f32),
                pltpu.VMEM((SECTIONS, extra, 2, own, gate), f32),
                pltpu.VMEM((len(CHAINED), extra, 8, own, gate), f32),
                pltpu.SemaphoreType.DMA((PHASES,)),
                pltpu.SemaphoreType.DMA((PHASES,)),
                pltpu.SemaphoreType.DMA((SECTIONS + len(CHAINED) if extra > 1 else 1, extra)),
                pltpu.SemaphoreType.DMA((SECTIONS + len(CHAINED) if extra > 1 else 1, extra)),
                pltpu.SemaphoreType.DMA((1,)),
            ],
            compiler_params=pltpu.CompilerParams(collective_id=0, has_side_effects=True),
            name="sweep",
        )(initial_state, adjoint_state, current_gates)
    )


def solution(mesh):
    return jax.shard_map(
        shards,
        mesh=mesh,
        in_specs=(
            P(None, ("groups", "long"), None),
            P(None, ("groups", "long"), None),
            P("groups", None, None, None),
        ),
        out_specs=(P(None, ("groups", "long"), None), P(None, ("groups", "long"), None)),
        check_vma=False,
    )
```

```python
import functools

import jax
import jax.numpy as jnp
from jax import lax
from jax.experimental import pallas as pl
from jax.experimental.pallas import tpu as pltpu
from jax.sharding import PartitionSpec as P

SECTIONS = 4
NS_ITERS = 8
MESH = pl.DeviceIdType.MESH
ADJ_IN, PSI_IN, ADJ_OUT, NEAR, HALF, FAR, FINAL, RS, AG, CROSS = 0, 1, 2, 3, 4, 5, 9, 17, 21, 25
CHAINED = (1, 2, 3)
CORE = CROSS + len(CHAINED)
PHASES = CORE + 2 * len(CHAINED)
BACK = ((0, 1), (), (), (), (2, 3))
SEND = (((), ()), ((), ()), ((2, 3), (0, 1)), ((), ()))


def split(x):
    high = x.astype(jnp.bfloat16)
    return high, (x - high.astype(jnp.float32)).astype(jnp.bfloat16)


def dot3(left, right, contract):
    def dot(a, b):
        return lax.dot_general(
            a, b, (contract, ((), ())), preferred_element_type=jnp.float32
        )

    return dot(left[0], right[0]) + (dot(left[0], right[1]) + dot(left[1], right[0]))


def embed_out(real, imag):
    return jnp.concatenate(
        [
            jnp.concatenate([real, -imag], axis=1),
            jnp.concatenate([imag, real], axis=1),
        ],
        axis=0,
    )


def swap_plane(plane, stride):
    rows, lanes = plane.shape
    rolled = pltpu.roll(plane, lanes // 2, 1)
    low = lax.broadcasted_iota(jnp.int32, (stride, lanes), 1) < lanes // 2
    blocks = []
    for start in range(0, rows, 2 * stride):
        mid, end = start + stride, start + 2 * stride
        blocks.append(jnp.where(low, plane[start:mid], rolled[mid:end]))
        blocks.append(jnp.where(low, rolled[start:mid], plane[mid:end]))
    return jnp.concatenate(blocks, axis=0)


def halves(x, q, per):
    stride = per << q
    starts = range(0, x.shape[0], 2 * stride)
    return [
        jnp.concatenate([x[k + bit * stride : k + (bit + 1) * stride] for k in starts], axis=0)
        for bit in range(2)
    ]


def swap_rows(x, stride):
    lanes = x.shape[1] // 2
    return jnp.concatenate(
        [swap_plane(x[:, :lanes], stride), swap_plane(x[:, lanes:], stride)], axis=1
    )


def swap(x, q, per):
    return swap_rows(x, per << q)


def embed(v):
    gate = v.shape[0]
    real, imag = v[:, :gate], v[:, gate:]
    return jnp.concatenate([v, jnp.concatenate([-imag, real], axis=1)], axis=0)


def contract_cross(cross, fitted):
    rows, gate = cross[0].shape
    half = gate // 2
    left = jnp.concatenate(
        [
            jnp.concatenate([cross[4 * u + 2 * v + plane] for u in range(2) for plane in range(2)], axis=1)
            for v in range(2)
        ],
        axis=0,
    )
    full = tuple(embed(x) for x in split(fitted))
    right = tuple(
        jnp.concatenate(
            [
                jnp.concatenate([x[u * half : (u + 1) * half], x[gate + u * half : gate + (u + 1) * half]], axis=0)
                for u in range(2)
            ],
            axis=1,
        )
        for x in full
    )
    out = dot3(split(left), right, ((1,), (1,)))
    low, high = out[:rows], out[rows:]
    return (
        jnp.concatenate([low[:, :half], high[:, :half]], axis=1),
        jnp.concatenate([low[:, half:], high[:, half:]], axis=1),
    )


def polar(x, sweeps):
    gate = x.shape[0]
    norm = lax.rsqrt(jnp.sum(x * x, keepdims=True) + 1e-06)

    def sweep(_, a):
        high, low = split(a)

        full = (embed(high), embed(low))
        def product(left, axis):
            def dot(u, v):
                return lax.dot_general(
                    u, v, (((1,), (axis,)), ((), ())), preferred_element_type=jnp.float32
                )

            both = dot(jnp.concatenate(left, axis=0), full[0])
            return both[:gate] + (both[gate:] + dot(left[0], full[1]))

        gram = product((high, low), 1)
        return 1.5 * a - 0.5 * product(split(gram), 0)

    return lax.fori_loop(0, sweeps, sweep, x * norm, unroll=8)


def kernel(
    used, order, extra_bits,
    psi_in, adj_in, gates_in, psi_out, adj_out,
    psi_buf, adj_buf, gates, phi_t, phi_cross, psi_send, adj_send,
    part, rs_buf, cross, pair_buf, chip_buf, cross_buf, ag_buf, final, half_gate, mid_buf, mid_cross,
    send_sem, recv_sem, mid_send, mid_recv, local_sem,
):
    group = lax.axis_index("groups")
    me = lax.axis_index("long")
    n = 2 ** len(used)
    extra = 2 ** len(extra_bits)
    rows = psi_in.shape[1]
    gate = psi_in.shape[2]
    owners = n // 2
    first = n // 4
    own = gate // owners
    per = rows // owners

    def gather(value, bits):
        out = 0
        for k, bit in enumerate(bits):
            out = out + lax.rem(lax.div(value, 2**bit), 2) * 2**k
        return out

    def scatter(value, bits):
        out = 0
        for k, bit in enumerate(bits):
            out = out + lax.rem(lax.div(value, 2**k), 2) * 2**bit
        return out

    slot = gather(me, used) if extra_bits else me
    layer = gather(me, extra_bits)

    def peer(j):
        return scatter(j, used) + scatter(layer, extra_bits) if extra_bits else j

    def layer_peer(j):
        return scatter(slot, used) + scatter(j, extra_bits)

    def others(fn, mine=slot, count=n):
        def step(off, carry):
            fn(lax.rem(mine + off, count))
            return carry

        lax.fori_loop(1, count, step, 0)

    quarter = n // 4
    column = lax.div(slot, quarter)
    upper = lax.div(column, 2)
    inner = column + upper * (3 - 2 * column)

    def far_first(fn, ranks=(0, 1, 2, 3)):
        for rank in ranks:
            place = (3, 2, 1 - inner, inner)[rank]
            base = (place + upper * (3 - 2 * place)) * quarter

            def step(k, carry):
                fn(base + lax.rem(slot + 1 + k, quarter))
                return carry

            for k in range(quarter - (rank == 3)):
                step(k, 0)

    def owners_far_first(fn, among=False):
        for rank in range(2):
            base = (2 - rank + upper * (2 * rank - 1)) * quarter

            def step(k, carry):
                fn(base + lax.rem(slot + 1 + k, quarter))
                return carry

            for k in range(quarter - rank):
                step(k, 0)

            if rank == 1 and not among:

                @pl.when(jnp.logical_not(is_owner))
                def _():
                    fn(base + lax.rem(slot, quarter))

    is_owner = inner == 1

    def remote(src, dst, phase, target):
        return pltpu.make_async_remote_copy(
            src_ref=src,
            dst_ref=dst,
            send_sem=send_sem.at[phase],
            recv_sem=recv_sem.at[phase],
            device_id={"groups": group, "long": target},
            device_id_type=MESH,
        )

    def block(ref, j, size):
        return ref.at[:, pl.ds(pl.multiple_of(j * size, size), size), :]

    def arrived(ref, phase):
        remote(ref, ref, phase, peer(lax.rem(slot + 1, n))).wait_recv()

    def departed(ref, phase):
        remote(ref, ref, phase, peer(lax.rem(slot + 1, n))).wait_send()

    index = slot - first

    def shard(k):
        return lax.rem(k, 2) * (owners // 2) + lax.div(k, 2)

    def signal(j, target):
        pl.semaphore_signal(
            barrier, inc=1, device_id={"groups": group, "long": target(j)}, device_id_type=MESH
        )

    barrier = pltpu.get_barrier_semaphore()

    @pl.when(is_owner)
    def _():
        far_first(lambda j: signal(j, peer))
        if extra > 1:
            others(lambda j: signal(j, layer_peer), layer, extra)
        pl.semaphore_wait(barrier, owners + extra - 2)

    @pl.when(jnp.logical_not(is_owner))
    def _():
        pl.semaphore_wait(barrier, owners)

    def inward(src, dst, phase):
        return lambda j: remote(block(src, j - first, per), block(dst, slot, per), phase, peer(j)).start()

    def outward(src, dst, phase):
        return lambda j: remote(block(src, j, per), block(dst, index, per), phase, peer(j)).start()

    def bit_of(q):
        return lax.rem(lax.div(slot, 2**q), 2)

    def flipped(q):
        return peer(slot + (1 - 2 * bit_of(q)) * 2**q)

    def variant(near, far):
        return near + 2 * far

    near_bit, far_bit = bit_of(order[2]), bit_of(order[3])
    mine_at = variant(near_bit, far_bit)
    other_at = variant(near_bit, 1 - far_bit)
    chunks = owners // 2
    chips = owners // 2
    wide = gate // 2
    pair = rows // chunks

    def target_variant(j):
        return variant(lax.rem(lax.div(j, 2 ** order[2]), 2), lax.rem(lax.div(j, 2 ** order[3]), 2))

    def to_final(j):
        remote(
            block(psi_send, j, per),
            block(final.at[target_variant(j)], index, per),
            FINAL + index,
            peer(j),
        ).start()

    def pass_across():
        def step(k, carry):
            part_k = lax.rem(k + upper * (owners // 2), owners)
            ref = block(final.at[mine_at], part_k, per)
            arrived(ref, FINAL + part_k)
            remote(ref, ref, FAR + lax.div(part_k, 2), flipped(order[3])).start()
            remote(ref, ref, NEAR, flipped(order[2])).start()
            return carry

        lax.fori_loop(0, owners, step, 0)

    def gather_final():
        def step(k, carry):
            part_k = lax.rem(k + upper * (chunks // 2), chunks)
            ref = block(final.at[other_at], part_k, pair)
            arrived(ref, FAR + part_k)
            remote(ref, ref, NEAR, flipped(order[2])).start()
            return carry

        lax.fori_loop(0, chunks, step, 0)
        arrived(final.at[pl.ds(0, 2)], NEAR)

    def keep_half(k, bit, x):
        half = gate // 2
        half_gate[k] = jnp.where(bit == 0, x[:half], x[half:])

    def fit(s):
        return polar(jnp.concatenate([ag_buf[s, 0], ag_buf[s, 1]], axis=1), NS_ITERS)

    def half_apply(x, k):
        full = embed_out(half_gate[k, :, :gate], half_gate[k, :, gate:])
        return dot3(split(x), split(full), ((1,), (1,)))

    def before_last():
        outs = []
        for far in range(2):
            both = [joined(final.at[variant(near, far)]) for near in range(2)]
            outs.append(half_apply(swap_rows(jnp.concatenate(both, axis=0), rows), 0))
        x = swap_plane(jnp.concatenate(outs, axis=0), 2 * rows)
        return jnp.concatenate([x[: 2 * rows], x[2 * rows :]], axis=1)

    def last(x):
        x = swap_plane(half_apply(x, 1), rows)
        psi_out[0] = x[:rows]
        psi_out[1] = x[rows:]

    def joined(ref):
        return jnp.concatenate([ref[0], ref[1]], axis=1)

    owners_far_first(inward(adj_in, adj_buf, ADJ_IN))
    owners_far_first(inward(psi_in, psi_buf, PSI_IN))

    def put(ref, x, done):
        for q in done[::-1]:
            x = swap(x, q, per)
        ref[0] = x[:, :gate]
        ref[1] = x[:, gate:]

    def advance_adjoint(phi, s):
        full = split(embed_out(gates[s, 0], gates[s, 1]))
        phi = dot3(split(phi), full, ((1,), (1,)))
        if s in CHAINED:
            for u, rows_u in enumerate(halves(phi, order[s], per)):
                high, low = split(rows_u.T)
                phi_cross[CHAINED.index(s), u, 0] = high
                phi_cross[CHAINED.index(s), u, 1] = low
        else:
            high, low = split(phi.T)
            phi_t[s, 0] = high
            phi_t[s, 1] = low
        return phi

    def outer(left, right):
        both = dot3(left, right, ((1,), (0,)))
        return both[:gate, :gate] + both[gate:, gate:], both[gate:, :gate] - both[:gate, gate:]

    def own_copy(src, dst, phase):
        return pltpu.make_async_copy(src, dst, recv_sem.at[phase])

    @pl.when(is_owner)
    def _():
        gate_copy = pltpu.make_async_copy(gates_in, gates, local_sem.at[0])
        gate_copy.start()
        own_copy(block(adj_in, index, per), block(adj_buf, slot, per), ADJ_IN).start()
        own_copy(block(psi_in, index, per), block(psi_buf, slot, per), PSI_IN).start()
        chip = lax.div(index, 2)
        parity = lax.rem(index, 2)
        mine = pl.ds(pl.multiple_of(shard(index) * own, own), own)

        gate_copy.wait()
        arrived(adj_buf, ADJ_IN)
        phi = joined(adj_buf)
        for s in range(SECTIONS):
            phi = advance_adjoint(swap(phi, order[s], per), s)
        put(adj_send, phi, order)
        own_copy(block(adj_send, slot, per), block(adj_out, index, per), ADJ_OUT).start()
        adj_back = outward(adj_send, adj_out, ADJ_OUT)
        for rank in BACK[SECTIONS]:
            far_first(adj_back, (rank,))
        arrived(psi_buf, PSI_IN)
        psi = swap(joined(psi_buf), order[0], per)
        fitted = None

        def among(fn):
            owners_far_first(fn, True)

        def over_layers(buf, total, kind):
            buf[layer] = total

            def across(j, here):
                return pltpu.make_async_remote_copy(
                    src_ref=buf.at[here],
                    dst_ref=buf.at[here],
                    send_sem=mid_send.at[kind, j],
                    recv_sem=mid_recv.at[kind, here],
                    device_id={"groups": group, "long": layer_peer(j)},
                    device_id_type=MESH,
                )

            others(lambda j: across(j, layer).start(), layer, extra)
            others(lambda j: across(j, j).wait_recv(), layer, extra)
            others(lambda j: across(j, layer).wait_send(), layer, extra)
            total = buf[0]
            for j in range(1, extra):
                total = total + buf[j]
            return total

        def reduced(src, buf, phase):
            arrived(buf.at[pl.ds(0, owners - 1)], phase)
            buf[index] = src[:, mine, :]
            total = buf[0]
            for j in range(1, owners):
                total = total + buf[j]
            return total

        def send_cross(k, u):
            planes = pl.ds(4 * u, 4)
            remote(
                block(cross.at[k, planes], 1 - parity, wide), pair_buf.at[k, planes], CORE + 2 * k + u, flipped(0)
            ).start()

        def pass_cross(k, u):
            planes = pl.ds(4 * u, 4)
            arrived(pair_buf.at[k, planes], CORE + 2 * k + u)
            rows_here = pl.ds(pl.multiple_of(parity * wide, wide), wide)
            chip_buf[k, planes] = cross[k, planes, rows_here, :] + pair_buf[k, planes]

            def step(off, carry):
                there = lax.rem(chip + off, chips)
                remote(
                    block(chip_buf.at[k, planes], there, own),
                    cross_buf.at[k, chip, planes],
                    CROSS + k,
                    peer(first + 2 * there + parity),
                ).start()
                return carry

            lax.fori_loop(1, chips, step, 0)

        def reduced_cross(k):
            arrived(cross_buf.at[k, pl.ds(0, chips - 1)], CROSS + k)
            cross_buf[k, chip] = chip_buf[k, :, pl.ds(pl.multiple_of(chip * own, own), own), :]
            total = cross_buf[k, 0]
            for j in range(1, chips):
                total = total + cross_buf[k, j]
            return total

        def send_plain(x, done):
            put(psi_send, x, done)
            pltpu.make_async_copy(
                block(psi_send, slot, per), block(final.at[mine_at], index, per), recv_sem.at[FINAL + index]
            ).start()

        def fill_cross(k, s, x):
            state = split(x)
            for u in range(2):
                for v in range(2):
                    right = tuple(halves(h, order[s + 1], per)[v] for h in state)
                    cross[k, 4 * u + 2 * v], cross[k, 4 * u + 2 * v + 1] = outer(
                        (phi_cross[k, u, 0], phi_cross[k, u, 1]), right
                    )
                send_cross(k, u)
            for u in range(2):
                pass_cross(k, u)

        def apply(x, gate_pair):
            return dot3(split(x), split(embed_out(gate_pair[:, :gate], gate_pair[:, gate:])), ((1,), (1,)))

        outer_peer = 3 * upper * quarter + lax.rem(slot, quarter)

        def share_half(k, bit, x):
            keep_half(k, bit, x)
            if k == 0:
                remote(half_gate.at[k], half_gate.at[k], HALF, peer(outer_peer)).start()

        for s in range(SECTIONS):
            ahead = CHAINED.index(s + 1) if s + 1 in CHAINED else None
            if s in CHAINED:
                k = CHAINED.index(s)
                total = reduced_cross(k)
                if extra > 1:
                    total = over_layers(mid_cross.at[k], total, SECTIONS + k)
                ag_buf[s, 0, mine, :], ag_buf[s, 1, mine, :] = contract_cross(total, fitted)
            else:
                part[s, 0], part[s, 1] = outer((phi_t[s, 0], phi_t[s, 1]), split(psi))
                among(
                    lambda j: remote(block(part.at[s], shard(j - first), own), rs_buf.at[s, index], RS + s, peer(j)).start()
                )
                if ahead is not None:
                    fill_cross(ahead, s, psi)
                if s == 2:
                    send_plain(psi, order[:3])
                for rank in SEND[s][0]:
                    far_first(to_final, (rank,))
                total = reduced(part.at[s], rs_buf.at[s], RS + s)
                if extra > 1:
                    total = over_layers(mid_buf.at[s], total, s)
                ag_buf[s, :, mine, :] = total
            held = block(ag_buf.at[s], shard(index), own)
            among(lambda j: remote(held, held, AG + s, peer(j)).start())
            if s == SECTIONS - 1:
                far_first(lambda j: remote(held, held, AG + s, peer(j)).start(), (0, 2))
            if s in CHAINED and s < SECTIONS - 1:
                plain = apply(psi, fitted)
                psi = swap(plain, order[s], per)
                if s == 2:
                    send_plain(plain, order[:2])
                for rank in SEND[s][0]:
                    far_first(to_final, (rank,))
                if ahead is not None:
                    fill_cross(ahead, s, psi)
            for rank in BACK[s]:
                far_first(adj_back, (rank,))
            for rank in SEND[s][1]:
                far_first(to_final, (rank,))
            if s == SECTIONS - 1:
                pass_across()
            arrived(block(ag_buf.at[s], 0, (owners - 1) * own), AG + s)
            fitted = fit(s)
            if s == SECTIONS - 2:
                share_half(0, near_bit, fitted)
            if s == SECTIONS - 1:
                share_half(1, far_bit, fitted)
            if ahead is None and s < SECTIONS - 1:
                psi = swap(apply(psi, fitted), order[s + 1], per)

        gather_final()
        last(before_last())
        for s in range(SECTIONS):
            sent = block(part.at[s], 0, (owners - 1) * own)
            departed(block(psi_send, 0, (n - 1) * own) if s == SECTIONS - 1 else sent, AG + s)
            if s in CHAINED:
                k = CHAINED.index(s)
                departed(block(chip_buf.at[k], 0, (chips - 1) * own), CROSS + k)
                for u in range(2):
                    departed(pair_buf.at[k, pl.ds(4 * u, 4)], CORE + 2 * k + u)
            else:
                departed(sent, RS + s)
        departed(block(adj_in, 0, (owners - 1) * per), ADJ_IN)
        departed(block(psi_in, 0, (owners - 1) * per), PSI_IN)
        departed(block(adj_send, 0, (n - 1) * per), ADJ_OUT)
        departed(block(psi_send, 0, (n - 1) * per), FINAL + index)
        departed(half_gate.at[0], HALF)

    @pl.when(jnp.logical_not(is_owner))
    def _():
        pass_across()
        gather_final()
        arrived(half_gate.at[0], HALF)
        x = before_last()
        arrived(ag_buf.at[SECTIONS - 1], AG + SECTIONS - 1)
        keep_half(1, far_bit, fit(SECTIONS - 1))
        last(x)
        departed(adj_in, ADJ_IN)
        departed(psi_in, PSI_IN)

    for k in range(chunks):
        departed(block(final.at[mine_at], 0, pair), FAR + k)
    departed(final.at[pl.ds(0, 2)], NEAR)
    arrived(adj_out, ADJ_OUT)


def shards(initial_state, adjoint_state, current_gates):
    bit_count = lax.axis_size("long").bit_length() - 1
    partner_bits = [bit_count - 1, bit_count // 2, 0, 1]
    used = sorted(set(partner_bits))
    assert len(used) == SECTIONS
    order = [used.index(bit) for bit in partner_bits]
    extra_bits = [bit for bit in range(bit_count) if bit not in used]
    n, extra = 2 ** len(used), 2 ** len(extra_bits)
    planes, rows, gate = initial_state.shape
    owners = n // 2
    own = gate // owners
    held = n * (rows // owners)
    f32, bf16 = jnp.float32, jnp.bfloat16
    anywhere = pl.BlockSpec(memory_space=pl.ANY)
    return tuple(
        pl.pallas_call(
            functools.partial(kernel, used, order, extra_bits),
            out_shape=[pltpu.VMEM(initial_state.shape, f32)] * 2,
            in_specs=[anywhere] * 3,
            out_specs=[pl.BlockSpec(memory_space=pltpu.VMEM)] * 2,
            scratch_shapes=[
                pltpu.VMEM((2, held, gate), f32),
                pltpu.VMEM((2, held, gate), f32),
                pltpu.VMEM(current_gates.shape, f32),
                pltpu.VMEM((SECTIONS, 2, 2 * gate, held), bf16),
                pltpu.VMEM((len(CHAINED), 2, 2, 2 * gate, held // 2), bf16),
                pltpu.VMEM((2, held, gate), f32),
                pltpu.VMEM((2, held, gate), f32),
                pltpu.VMEM((SECTIONS, 2, gate, gate), f32),
                pltpu.VMEM((SECTIONS, owners, 2, own, gate), f32),
                pltpu.VMEM((len(CHAINED), 8, gate, gate), f32),
                pltpu.VMEM((len(CHAINED), 8, gate // 2, gate), f32),
                pltpu.VMEM((len(CHAINED), 8, gate // 2, gate), f32),
                pltpu.VMEM((len(CHAINED), owners // 2, 8, own, gate), f32),
                pltpu.VMEM((SECTIONS, 2, gate, gate), f32),
                pltpu.VMEM((4, planes, rows, gate), f32),
                pltpu.VMEM((2, gate // 2, 2 * gate), f32),
                pltpu.VMEM((SECTIONS, extra, 2, own, gate), f32),
                pltpu.VMEM((len(CHAINED), extra, 8, own, gate), f32),
                pltpu.SemaphoreType.DMA((PHASES,)),
                pltpu.SemaphoreType.DMA((PHASES,)),
                pltpu.SemaphoreType.DMA((SECTIONS + len(CHAINED) if extra > 1 else 1, extra)),
                pltpu.SemaphoreType.DMA((SECTIONS + len(CHAINED) if extra > 1 else 1, extra)),
                pltpu.SemaphoreType.DMA((1,)),
            ],
            compiler_params=pltpu.CompilerParams(collective_id=0, has_side_effects=True),
            name="sweep",
        )(initial_state, adjoint_state, current_gates)
    )


def solution(mesh):
    return jax.shard_map(
        shards,
        mesh=mesh,
        in_specs=(
            P(None, ("groups", "long"), None),
            P(None, ("groups", "long"), None),
            P("groups", None, None, None),
        ),
        out_specs=(P(None, ("groups", "long"), None), P(None, ("groups", "long"), None)),
        check_vma=False,
    )
```

```python
import functools

import jax
import jax.numpy as jnp
from jax import lax
from jax.experimental import pallas as pl
from jax.experimental.pallas import tpu as pltpu
from jax.sharding import PartitionSpec as P

SECTIONS = 4
NS_ITERS = 8
MESH = pl.DeviceIdType.MESH
ADJ_IN, PSI_IN, ADJ_OUT, NEAR, HALF, FAR, FINAL, RS, AG, EXTRA, MIRROR, CROSS = 0, 1, 2, 3, 4, 5, 9, 17, 21, 25, 26, 27
CHAINED = (1, 2, 3)
CORE = CROSS + len(CHAINED)
PHASES = CORE + 2 * len(CHAINED)
BACK = ((), (0,), (1,), (), (2, 3))
SEND = (((), ()), ((), ()), ((2, 3), ()), ((), ()))


def split(x):
    high = x.astype(jnp.bfloat16)
    return high, (x - high.astype(jnp.float32)).astype(jnp.bfloat16)


def dot3(left, right, contract):
    def dot(a, b):
        return lax.dot_general(
            a, b, (contract, ((), ())), preferred_element_type=jnp.float32
        )

    return dot(left[0], right[0]) + (dot(left[0], right[1]) + dot(left[1], right[0]))


def embed_out(real, imag):
    return jnp.concatenate(
        [
            jnp.concatenate([real, -imag], axis=1),
            jnp.concatenate([imag, real], axis=1),
        ],
        axis=0,
    )


def swap_plane(plane, stride):
    rows, lanes = plane.shape
    rolled = pltpu.roll(plane, lanes // 2, 1)
    low = lax.broadcasted_iota(jnp.int32, (stride, lanes), 1) < lanes // 2
    blocks = []
    for start in range(0, rows, 2 * stride):
        mid, end = start + stride, start + 2 * stride
        blocks.append(jnp.where(low, plane[start:mid], rolled[mid:end]))
        blocks.append(jnp.where(low, rolled[start:mid], plane[mid:end]))
    return jnp.concatenate(blocks, axis=0)


def halves(x, q, per):
    stride = per << q
    starts = range(0, x.shape[0], 2 * stride)
    return [
        jnp.concatenate([x[k + bit * stride : k + (bit + 1) * stride] for k in starts], axis=0)
        for bit in range(2)
    ]


def swap_rows(x, stride):
    lanes = x.shape[1] // 2
    return jnp.concatenate(
        [swap_plane(x[:, :lanes], stride), swap_plane(x[:, lanes:], stride)], axis=1
    )


def swap(x, q, per):
    return swap_rows(x, per << q)


def embed(v):
    gate = v.shape[0]
    real, imag = v[:, :gate], v[:, gate:]
    return jnp.concatenate([v, jnp.concatenate([-imag, real], axis=1)], axis=0)


def contract_cross(cross, fitted):
    rows, gate = cross[0].shape
    half = gate // 2
    left = jnp.concatenate(
        [
            jnp.concatenate([cross[4 * u + 2 * v + plane] for u in range(2) for plane in range(2)], axis=1)
            for v in range(2)
        ],
        axis=0,
    )
    full = tuple(embed(x) for x in split(fitted))
    right = tuple(
        jnp.concatenate(
            [
                jnp.concatenate([x[u * half : (u + 1) * half], x[gate + u * half : gate + (u + 1) * half]], axis=0)
                for u in range(2)
            ],
            axis=1,
        )
        for x in full
    )
    out = dot3(split(left), right, ((1,), (1,)))
    low, high = out[:rows], out[rows:]
    return (
        jnp.concatenate([low[:, :half], high[:, :half]], axis=1),
        jnp.concatenate([low[:, half:], high[:, half:]], axis=1),
    )


def polar(x, sweeps):
    gate = x.shape[0]
    norm = lax.rsqrt(jnp.sum(x * x, keepdims=True) + 1e-06)

    def sweep(_, a):
        high, low = split(a)

        full = (embed(high), embed(low))
        def product(left, axis):
            def dot(u, v):
                return lax.dot_general(
                    u, v, (((1,), (axis,)), ((), ())), preferred_element_type=jnp.float32
                )

            both = dot(jnp.concatenate(left, axis=0), full[0])
            return both[:gate] + (both[gate:] + dot(left[0], full[1]))

        gram = product((high, low), 1)
        return 1.5 * a - 0.5 * product(split(gram), 0)

    return lax.fori_loop(0, sweeps, sweep, x * norm, unroll=8)


def kernel(
    used, order, extra_bits,
    psi_in, adj_in, gates_in, psi_out, adj_out,
    psi_buf, adj_buf, gates, phi_t, phi_cross, psi_send, adj_send,
    psi_twin, twin_send, part, rs_buf, cross, pair_buf, chip_buf, cross_buf, ag_buf, final, half_gate, mid_buf, mid_cross,
    send_sem, recv_sem, mid_send, mid_recv, local_sem,
):
    group = lax.axis_index("groups")
    me = lax.axis_index("long")
    n = 2 ** len(used)
    extra = 2 ** len(extra_bits)
    rows = psi_in.shape[1]
    gate = psi_in.shape[2]
    owners = n // 2
    first = n // 4
    own = gate // owners
    per = rows // owners

    def gather(value, bits):
        out = 0
        for k, bit in enumerate(bits):
            out = out + lax.rem(lax.div(value, 2**bit), 2) * 2**k
        return out

    def scatter(value, bits):
        out = 0
        for k, bit in enumerate(bits):
            out = out + lax.rem(lax.div(value, 2**k), 2) * 2**bit
        return out

    slot = gather(me, used) if extra_bits else me
    layer = gather(me, extra_bits)

    def peer(j):
        return scatter(j, used) + scatter(layer, extra_bits) if extra_bits else j

    def layer_peer(j):
        return scatter(slot, used) + scatter(j, extra_bits)

    def others(fn, mine=slot, count=n):
        def step(off, carry):
            fn(lax.rem(mine + off, count))
            return carry

        lax.fori_loop(1, count, step, 0)

    quarter = n // 4
    column = lax.div(slot, quarter)
    upper = lax.div(column, 2)
    inner = column + upper * (3 - 2 * column)

    def far_first(fn, ranks=(0, 1, 2, 3)):
        for rank in ranks:
            place = (3, 2, 1 - inner, inner)[rank]
            base = (place + upper * (3 - 2 * place)) * quarter

            def step(k, carry):
                fn(base + lax.rem(slot + 1 + k, quarter))
                return carry

            for k in range(quarter - (rank == 3)):
                step(k, 0)

    def owners_far_first(fn, among=False):
        for rank in range(2):
            base = (2 - rank + upper * (2 * rank - 1)) * quarter

            def step(k, carry):
                fn(base + lax.rem(slot + 1 + k, quarter))
                return carry

            for k in range(quarter - rank):
                step(k, 0)

            if rank == 1 and not among:

                @pl.when(jnp.logical_not(is_owner))
                def _():
                    fn(base + lax.rem(slot, quarter))

    is_owner = inner == 1

    def remote(src, dst, phase, target):
        return pltpu.make_async_remote_copy(
            src_ref=src,
            dst_ref=dst,
            send_sem=send_sem.at[phase],
            recv_sem=recv_sem.at[phase],
            device_id={"groups": group, "long": target},
            device_id_type=MESH,
        )

    def block(ref, j, size):
        return ref.at[:, pl.ds(pl.multiple_of(j * size, size), size), :]

    def arrived(ref, phase):
        remote(ref, ref, phase, peer(lax.rem(slot + 1, n))).wait_recv()

    def departed(ref, phase):
        remote(ref, ref, phase, peer(lax.rem(slot + 1, n))).wait_send()

    index = slot - first

    def shard(k):
        return lax.rem(k, 2) * (owners // 2) + lax.div(k, 2)

    def signal(j, target):
        pl.semaphore_signal(
            barrier, inc=1, device_id={"groups": group, "long": target(j)}, device_id_type=MESH
        )

    barrier = pltpu.get_barrier_semaphore()

    @pl.when(is_owner)
    def _():
        far_first(lambda j: signal(j, peer))
        if extra > 1:
            others(lambda j: signal(j, layer_peer), layer, extra)
        pl.semaphore_wait(barrier, owners + extra - 2)

    @pl.when(jnp.logical_not(is_owner))
    def _():
        pl.semaphore_wait(barrier, owners)

    def inward(src, dst, phase):
        return lambda j: remote(block(src, j - first, per), block(dst, slot, per), phase, peer(j)).start()

    def outward(src, dst, phase):
        return lambda j: remote(block(src, j, per), block(dst, index, per), phase, peer(j)).start()

    def bit_of(q):
        return lax.rem(lax.div(slot, 2**q), 2)

    def flipped(q):
        return peer(slot + (1 - 2 * bit_of(q)) * 2**q)

    def variant(near, far):
        return near + 2 * far

    near_bit, far_bit = bit_of(order[2]), bit_of(order[3])
    mine_at = variant(near_bit, far_bit)
    other_at = variant(near_bit, 1 - far_bit)
    chunks = owners // 2
    chips = owners // 2
    wide = gate // 2
    pair = rows // chunks

    def target_variant(j):
        return variant(lax.rem(lax.div(j, 2 ** order[2]), 2), lax.rem(lax.div(j, 2 ** order[3]), 2))

    def to_final(src, at, j):
        there = j + (far_bit - lax.rem(lax.div(j, 2 ** order[3]), 2)) * 2 ** order[3]
        remote(src(j), block(final.at[target_variant(j)], at, per), FINAL + at, peer(there)).start()

    def to_final_chip(src, at):
        for far in range(2):
            j = slot + (far - far_bit) * 2 ** order[3]
            pltpu.make_async_copy(
                src(j),
                block(final.at[variant(near_bit, far)], at, per),
                recv_sem.at[FINAL + at],
            ).start()
            to_final(src, at, j + (1 - 2 * near_bit) * 2 ** order[2])

    def to_final_side(src, at):
        far_first(lambda j: to_final(src, at, j), (2,))
        to_final_chip(src, at)

    def over_slices(fn, side_far):
        def step(k, carry):
            half = lax.rem(lax.div(k, 2) + upper, 2)
            fn(2 * half + lax.rem(k, 2), 4 * half + 2 * side_far + lax.rem(k, 2))
            return carry

        lax.fori_loop(0, chunks, step, 0)

    def slices(k):
        return [block(final.at[variant(near_bit, far)], k, per) for far in range(2)]

    def two_blocks():
        return block(final.at[mine_at], 0, pair)

    def pass_across():
        def step(chunk, k):
            arrived(two_blocks(), FINAL + k)
            for ref in slices(k):
                remote(ref, ref, FAR + chunk, flipped(order[3])).start()
            for ref in slices(k):
                remote(ref, ref, NEAR, flipped(order[2])).start()

        over_slices(step, far_bit)

    def gather_final():
        def step(chunk, k):
            arrived(two_blocks(), FAR + chunk)
            for ref in slices(k):
                remote(ref, ref, NEAR, flipped(order[2])).start()

        over_slices(step, 1 - far_bit)
        arrived(final.at[pl.ds(0, 2)], NEAR)

    def keep_half(k, bit, x):
        half = gate // 2
        half_gate[k] = jnp.where(bit == 0, x[:half], x[half:])

    def fit(s):
        return polar(jnp.concatenate([ag_buf[s, 0], ag_buf[s, 1]], axis=1), NS_ITERS)

    def half_apply(x, k):
        full = embed_out(half_gate[k, :, :gate], half_gate[k, :, gate:])
        return dot3(split(x), split(full), ((1,), (1,)))

    def before_last():
        outs = []
        for far in range(2):
            both = [joined(final.at[variant(near, far)]) for near in range(2)]
            outs.append(half_apply(swap_rows(jnp.concatenate(both, axis=0), rows), 0))
        x = swap_plane(jnp.concatenate(outs, axis=0), 2 * rows)
        return jnp.concatenate([x[: 2 * rows], x[2 * rows :]], axis=1)

    def last(x):
        x = swap_plane(half_apply(x, 1), rows)
        psi_out[0] = x[:rows]
        psi_out[1] = x[rows:]

    def joined(ref):
        return jnp.concatenate([ref[0], ref[1]], axis=1)

    owners_far_first(inward(adj_in, adj_buf, ADJ_IN))
    owners_far_first(inward(psi_in, psi_buf, PSI_IN))

    def twin(k):
        return lax.rem(k + owners // 2, owners)

    side = first + upper * (owners // 2)
    half_held = n * per // 2

    def near_owners(fn):
        for k in range(1, owners // 2 + 1):
            j = side + lax.rem(slot + k, owners // 2)
            if k < owners // 2:
                fn(j)
            else:

                @pl.when(jnp.logical_not(is_owner))
                def _():
                    fn(j)

    near_owners(
        lambda j: remote(
            block(psi_in, twin(j - first), per), block(psi_twin, slot, per), EXTRA, peer(j)
        ).start()
    )

    def put(ref, x, done):
        for q in done[::-1]:
            x = swap(x, q, per)
        ref[0] = x[:, :gate]
        ref[1] = x[:, gate:]

    def advance_adjoint(phi, s):
        full = split(embed_out(gates[s, 0], gates[s, 1]))
        phi = dot3(split(phi), full, ((1,), (1,)))
        if s in CHAINED:
            for u, rows_u in enumerate(halves(phi, order[s], per)):
                high, low = split(rows_u.T)
                phi_cross[CHAINED.index(s), u, 0] = high
                phi_cross[CHAINED.index(s), u, 1] = low
        else:
            high, low = split(phi.T)
            phi_t[s, 0] = high
            phi_t[s, 1] = low
        return phi

    def outer(left, right):
        both = dot3(left, right, ((1,), (0,)))
        return both[:gate, :gate] + both[gate:, gate:], both[gate:, :gate] - both[:gate, gate:]

    def own_copy(src, dst, phase):
        return pltpu.make_async_copy(src, dst, recv_sem.at[phase])

    @pl.when(is_owner)
    def _():
        gate_copy = pltpu.make_async_copy(gates_in, gates, local_sem.at[0])
        gate_copy.start()
        own_copy(block(adj_in, index, per), block(adj_buf, slot, per), ADJ_IN).start()
        own_copy(block(psi_in, index, per), block(psi_buf, slot, per), PSI_IN).start()
        own_copy(block(psi_in, twin(index), per), block(psi_twin, slot, per), EXTRA).start()
        chip = lax.div(index, 2)
        parity = lax.rem(index, 2)
        mine = pl.ds(pl.multiple_of(shard(index) * own, own), own)

        gate_copy.wait()
        arrived(adj_buf, ADJ_IN)
        phi = joined(adj_buf)
        for s in range(SECTIONS):
            phi = advance_adjoint(swap(phi, order[s], per), s)
        put(adj_send, phi, order)
        own_copy(block(adj_send, slot, per), block(adj_out, index, per), ADJ_OUT).start()
        adj_back = outward(adj_send, adj_out, ADJ_OUT)
        for rank in BACK[SECTIONS]:
            far_first(adj_back, (rank,))
        arrived(psi_buf, PSI_IN)
        psi = swap(joined(psi_buf), order[0], per)
        fitted = None

        def among(fn):
            owners_far_first(fn, True)

        def over_layers(buf, total, kind):
            buf[layer] = total

            def across(j, here):
                return pltpu.make_async_remote_copy(
                    src_ref=buf.at[here],
                    dst_ref=buf.at[here],
                    send_sem=mid_send.at[kind, j],
                    recv_sem=mid_recv.at[kind, here],
                    device_id={"groups": group, "long": layer_peer(j)},
                    device_id_type=MESH,
                )

            others(lambda j: across(j, layer).start(), layer, extra)
            others(lambda j: across(j, j).wait_recv(), layer, extra)
            others(lambda j: across(j, layer).wait_send(), layer, extra)
            total = buf[0]
            for j in range(1, extra):
                total = total + buf[j]
            return total

        def reduced(src, buf, phase):
            arrived(buf.at[pl.ds(0, owners - 1)], phase)
            buf[index] = src[:, mine, :]
            total = buf[0]
            for j in range(1, owners):
                total = total + buf[j]
            return total

        def send_cross(k, u):
            planes = pl.ds(4 * u, 4)
            remote(
                block(cross.at[k, planes], 1 - parity, wide), pair_buf.at[k, planes], CORE + 2 * k + u, flipped(0)
            ).start()

        def pass_cross(k, u):
            planes = pl.ds(4 * u, 4)
            arrived(pair_buf.at[k, planes], CORE + 2 * k + u)
            rows_here = pl.ds(pl.multiple_of(parity * wide, wide), wide)
            chip_buf[k, planes] = cross[k, planes, rows_here, :] + pair_buf[k, planes]

            def step(off, carry):
                there = lax.rem(chip + off, chips)
                remote(
                    block(chip_buf.at[k, planes], there, own),
                    cross_buf.at[k, chip, planes],
                    CROSS + k,
                    peer(first + 2 * there + parity),
                ).start()
                return carry

            lax.fori_loop(1, chips, step, 0)

        def reduced_cross(k):
            arrived(cross_buf.at[k, pl.ds(0, chips - 1)], CROSS + k)
            cross_buf[k, chip] = chip_buf[k, :, pl.ds(pl.multiple_of(chip * own, own), own), :]
            total = cross_buf[k, 0]
            for j in range(1, chips):
                total = total + cross_buf[k, j]
            return total

        def twin_first(u):
            arrived(block(psi_twin, 0, half_held), EXTRA)
            arrived(block(psi_twin, 0, half_held), MIRROR)
            x = swap(apply(swap(joined(psi_twin), order[0], per), u), order[0], per)
            return jnp.where(upper == 0, x[:half_held], x[half_held:])

        def send_twin(x, u):
            x = swap(apply(swap(x, order[1], per), u), order[1], per)
            twin_send[0] = x[:, :gate]
            twin_send[1] = x[:, gate:]
            at = twin(index)

            to_final_side(lambda j: block(twin_send, j - upper * (n // 2), per), at)

        def send_plain(x, done):
            put(psi_send, x, done)
            to_final_side(lambda j: block(psi_send, j, per), index)

        def fill_cross(k, s, x):
            state = split(x)
            for u in range(2):
                for v in range(2):
                    right = tuple(halves(h, order[s + 1], per)[v] for h in state)
                    cross[k, 4 * u + 2 * v], cross[k, 4 * u + 2 * v + 1] = outer(
                        (phi_cross[k, u, 0], phi_cross[k, u, 1]), right
                    )
                send_cross(k, u)
            for u in range(2):
                pass_cross(k, u)

        def apply(x, gate_pair):
            return dot3(split(x), split(embed_out(gate_pair[:, :gate], gate_pair[:, gate:])), ((1,), (1,)))

        outer_peer = 3 * upper * quarter + lax.rem(slot, quarter)

        def share_half(k, bit, x):
            keep_half(k, bit, x)
            if k == 0:
                remote(half_gate.at[k], half_gate.at[k], HALF, peer(outer_peer)).start()

        for s in range(SECTIONS):
            ahead = CHAINED.index(s + 1) if s + 1 in CHAINED else None
            if s in CHAINED:
                k = CHAINED.index(s)
                total = reduced_cross(k)
                if extra > 1:
                    total = over_layers(mid_cross.at[k], total, SECTIONS + k)
                ag_buf[s, 0, mine, :], ag_buf[s, 1, mine, :] = contract_cross(total, fitted)
            else:
                part[s, 0], part[s, 1] = outer((phi_t[s, 0], phi_t[s, 1]), split(psi))
                among(
                    lambda j: remote(block(part.at[s], shard(j - first), own), rs_buf.at[s, index], RS + s, peer(j)).start()
                )
                if ahead is not None:
                    fill_cross(ahead, s, psi)
                if s == 2:
                    send_plain(psi, order[:3])
                total = reduced(part.at[s], rs_buf.at[s], RS + s)
                if extra > 1:
                    total = over_layers(mid_buf.at[s], total, s)
                ag_buf[s, :, mine, :] = total
            held = block(ag_buf.at[s], shard(index), own)
            among(lambda j: remote(held, held, AG + s, peer(j)).start())
            if s == SECTIONS - 1:
                far_first(lambda j: remote(held, held, AG + s, peer(j)).start(), (0, 2))
            if s in CHAINED and s < SECTIONS - 1:
                plain = apply(psi, fitted)
                psi = swap(plain, order[s], per)
                if s == 2:
                    send_plain(plain, order[:2])
                if ahead is not None:
                    fill_cross(ahead, s, psi)
                if s == 2:
                    send_twin(twin_state, fitted)
            for rank in BACK[s]:
                far_first(adj_back, (rank,))
            if s == SECTIONS - 1:
                pass_across()
            arrived(block(ag_buf.at[s], 0, (owners - 1) * own), AG + s)
            if s == 0:
                theirs = block(psi_buf, upper, half_held)
                remote(theirs, block(psi_twin, upper, half_held), MIRROR, peer(first + twin(index))).start()
            if s == 1:
                twin_state = twin_first(fitted)
            fitted = fit(s)
            if s == SECTIONS - 2:
                share_half(0, near_bit, fitted)
            if s == SECTIONS - 1:
                share_half(1, far_bit, fitted)
            if ahead is None and s < SECTIONS - 1:
                psi = swap(apply(psi, fitted), order[s + 1], per)

        gather_final()
        last(before_last())
        for s in range(SECTIONS):
            sent = block(part.at[s], 0, (owners - 1) * own)
            departed(block(psi_send, 0, (n - 1) * own) if s == SECTIONS - 1 else sent, AG + s)
            if s in CHAINED:
                k = CHAINED.index(s)
                departed(block(chip_buf.at[k], 0, (chips - 1) * own), CROSS + k)
                for u in range(2):
                    departed(pair_buf.at[k, pl.ds(4 * u, 4)], CORE + 2 * k + u)
            else:
                departed(sent, RS + s)
        departed(block(adj_in, 0, (owners - 1) * per), ADJ_IN)
        departed(block(psi_in, 0, (owners - 1) * per), PSI_IN)
        departed(block(adj_send, 0, (n - 1) * per), ADJ_OUT)
        departed(block(psi_send, 0, (n // 2 - 2) * per), FINAL + index)
        departed(block(psi_send, 0, (n // 2 - 2) * per), FINAL + twin(index))
        departed(block(psi_in, 0, (owners // 2 - 1) * per), EXTRA)
        departed(block(psi_twin, 0, half_held), MIRROR)
        departed(half_gate.at[0], HALF)

    @pl.when(jnp.logical_not(is_owner))
    def _():
        pass_across()
        gather_final()
        arrived(half_gate.at[0], HALF)
        x = before_last()
        arrived(ag_buf.at[SECTIONS - 1], AG + SECTIONS - 1)
        keep_half(1, far_bit, fit(SECTIONS - 1))
        last(x)
        departed(adj_in, ADJ_IN)
        departed(psi_in, PSI_IN)
        departed(block(psi_in, 0, owners // 2 * per), EXTRA)

    for k in range(chunks):
        departed(block(final.at[mine_at], 0, pair), FAR + k)
    departed(final.at[pl.ds(0, 2)], NEAR)
    arrived(adj_out, ADJ_OUT)


def shards(initial_state, adjoint_state, current_gates):
    bit_count = lax.axis_size("long").bit_length() - 1
    partner_bits = [bit_count - 1, bit_count // 2, 0, 1]
    used = sorted(set(partner_bits))
    assert len(used) == SECTIONS
    order = [used.index(bit) for bit in partner_bits]
    extra_bits = [bit for bit in range(bit_count) if bit not in used]
    n, extra = 2 ** len(used), 2 ** len(extra_bits)
    planes, rows, gate = initial_state.shape
    owners = n // 2
    own = gate // owners
    held = n * (rows // owners)
    f32, bf16 = jnp.float32, jnp.bfloat16
    anywhere = pl.BlockSpec(memory_space=pl.ANY)
    return tuple(
        pl.pallas_call(
            functools.partial(kernel, used, order, extra_bits),
            out_shape=[pltpu.VMEM(initial_state.shape, f32)] * 2,
            in_specs=[anywhere] * 3,
            out_specs=[pl.BlockSpec(memory_space=pltpu.VMEM)] * 2,
            scratch_shapes=[
                pltpu.VMEM((2, held, gate), f32),
                pltpu.VMEM((2, held, gate), f32),
                pltpu.VMEM(current_gates.shape, f32),
                pltpu.VMEM((SECTIONS, 2, 2 * gate, held), bf16),
                pltpu.VMEM((len(CHAINED), 2, 2, 2 * gate, held // 2), bf16),
                pltpu.VMEM((2, held, gate), f32),
                pltpu.VMEM((2, held, gate), f32),
                pltpu.VMEM((2, held, gate), f32),
                pltpu.VMEM((2, held // 2, gate), f32),
                pltpu.VMEM((SECTIONS, 2, gate, gate), f32),
                pltpu.VMEM((SECTIONS, owners, 2, own, gate), f32),
                pltpu.VMEM((len(CHAINED), 8, gate, gate), f32),
                pltpu.VMEM((len(CHAINED), 8, gate // 2, gate), f32),
                pltpu.VMEM((len(CHAINED), 8, gate // 2, gate), f32),
                pltpu.VMEM((len(CHAINED), owners // 2, 8, own, gate), f32),
                pltpu.VMEM((SECTIONS, 2, gate, gate), f32),
                pltpu.VMEM((4, planes, rows, gate), f32),
                pltpu.VMEM((2, gate // 2, 2 * gate), f32),
                pltpu.VMEM((SECTIONS, extra, 2, own, gate), f32),
                pltpu.VMEM((len(CHAINED), extra, 8, own, gate), f32),
                pltpu.SemaphoreType.DMA((PHASES,)),
                pltpu.SemaphoreType.DMA((PHASES,)),
                pltpu.SemaphoreType.DMA((SECTIONS + len(CHAINED) if extra > 1 else 1, extra)),
                pltpu.SemaphoreType.DMA((SECTIONS + len(CHAINED) if extra > 1 else 1, extra)),
                pltpu.SemaphoreType.DMA((1,)),
            ],
            compiler_params=pltpu.CompilerParams(collective_id=0, has_side_effects=True),
            name="sweep",
        )(initial_state, adjoint_state, current_gates)
    )


def solution(mesh):
    return jax.shard_map(
        shards,
        mesh=mesh,
        in_specs=(
            P(None, ("groups", "long"), None),
            P(None, ("groups", "long"), None),
            P("groups", None, None, None),
        ),
        out_specs=(P(None, ("groups", "long"), None), P(None, ("groups", "long"), None)),
        check_vma=False,
    )
```

```python
import functools

import jax
import jax.numpy as jnp
from jax import lax
from jax.experimental import pallas as pl
from jax.experimental.pallas import tpu as pltpu
from jax.sharding import PartitionSpec as P

SECTIONS = 4
NS_ITERS = 8
MESH = pl.DeviceIdType.MESH
ADJ_IN, PSI_IN, ADJ_OUT, NEAR, HALF, FAR, FINAL, RS, AG, EXTRA, MIRROR, CROSS = 0, 1, 2, 3, 4, 5, 9, 17, 21, 25, 26, 27
CHAINED = (1, 2, 3)
CORE = CROSS + len(CHAINED)
PHASES = CORE + 2 * len(CHAINED)
BACK = ((), (0,), (1,), (), (2, 3))
SEND = (((), ()), ((), ()), ((2, 3), ()), ((), ()))


def split(x):
    high = x.astype(jnp.bfloat16)
    return high, (x - high.astype(jnp.float32)).astype(jnp.bfloat16)


def dot3(left, right, contract):
    def dot(a, b):
        return lax.dot_general(
            a, b, (contract, ((), ())), preferred_element_type=jnp.float32
        )

    return dot(left[0], right[0]) + (dot(left[0], right[1]) + dot(left[1], right[0]))


def embed_out(real, imag):
    return jnp.concatenate(
        [
            jnp.concatenate([real, -imag], axis=1),
            jnp.concatenate([imag, real], axis=1),
        ],
        axis=0,
    )


def swap_plane(plane, stride):
    rows, lanes = plane.shape
    rolled = pltpu.roll(plane, lanes // 2, 1)
    low = lax.broadcasted_iota(jnp.int32, (stride, lanes), 1) < lanes // 2
    blocks = []
    for start in range(0, rows, 2 * stride):
        mid, end = start + stride, start + 2 * stride
        blocks.append(jnp.where(low, plane[start:mid], rolled[mid:end]))
        blocks.append(jnp.where(low, rolled[start:mid], plane[mid:end]))
    return jnp.concatenate(blocks, axis=0)


def halves(x, q, per):
    stride = per << q
    starts = range(0, x.shape[0], 2 * stride)
    return [
        jnp.concatenate([x[k + bit * stride : k + (bit + 1) * stride] for k in starts], axis=0)
        for bit in range(2)
    ]


def swap_rows(x, stride):
    lanes = x.shape[1] // 2
    return jnp.concatenate(
        [swap_plane(x[:, :lanes], stride), swap_plane(x[:, lanes:], stride)], axis=1
    )


def swap(x, q, per):
    return swap_rows(x, per << q)


def embed(v):
    gate = v.shape[0]
    real, imag = v[:, :gate], v[:, gate:]
    return jnp.concatenate([v, jnp.concatenate([-imag, real], axis=1)], axis=0)


def contract_cross(cross, fitted):
    rows, gate = cross[0].shape
    half = gate // 2
    left = jnp.concatenate(
        [
            jnp.concatenate([cross[4 * u + 2 * v + plane] for u in range(2) for plane in range(2)], axis=1)
            for v in range(2)
        ],
        axis=0,
    )
    full = tuple(embed(x) for x in split(fitted))
    right = tuple(
        jnp.concatenate(
            [
                jnp.concatenate([x[u * half : (u + 1) * half], x[gate + u * half : gate + (u + 1) * half]], axis=0)
                for u in range(2)
            ],
            axis=1,
        )
        for x in full
    )
    out = dot3(split(left), right, ((1,), (1,)))
    low, high = out[:rows], out[rows:]
    return (
        jnp.concatenate([low[:, :half], high[:, :half]], axis=1),
        jnp.concatenate([low[:, half:], high[:, half:]], axis=1),
    )


def polar(x, sweeps):
    gate = x.shape[0]
    norm = lax.rsqrt(jnp.sum(x * x, keepdims=True) + 1e-06)

    def sweep(_, a):
        high, low = split(a)

        full = (embed(high), embed(low))
        def product(left, axis):
            def dot(u, v):
                return lax.dot_general(
                    u, v, (((1,), (axis,)), ((), ())), preferred_element_type=jnp.float32
                )

            both = dot(jnp.concatenate(left, axis=0), full[0])
            return both[:gate] + (both[gate:] + dot(left[0], full[1]))

        gram = product((high, low), 1)
        return 1.5 * a - 0.5 * product(split(gram), 0)

    return lax.fori_loop(0, sweeps, sweep, x * norm, unroll=8)


def kernel(
    used, order, extra_bits,
    psi_in, adj_in, gates_in, psi_out, adj_out,
    psi_buf, adj_buf, gates, phi_t, phi_cross, psi_send, adj_send,
    psi_twin, twin_send, part, rs_buf, cross, pair_buf, chip_buf, cross_buf, ag_buf, final, half_gate, mid_buf, mid_cross,
    send_sem, recv_sem, mid_send, mid_recv, local_sem,
):
    group = lax.axis_index("groups")
    me = lax.axis_index("long")
    n = 2 ** len(used)
    extra = 2 ** len(extra_bits)
    rows = psi_in.shape[1]
    gate = psi_in.shape[2]
    owners = n // 2
    first = n // 4
    own = gate // owners
    per = rows // owners

    def gather(value, bits):
        out = 0
        for k, bit in enumerate(bits):
            out = out + lax.rem(lax.div(value, 2**bit), 2) * 2**k
        return out

    def scatter(value, bits):
        out = 0
        for k, bit in enumerate(bits):
            out = out + lax.rem(lax.div(value, 2**k), 2) * 2**bit
        return out

    slot = gather(me, used) if extra_bits else me
    layer = gather(me, extra_bits)

    def peer(j):
        return scatter(j, used) + scatter(layer, extra_bits) if extra_bits else j

    def layer_peer(j):
        return scatter(slot, used) + scatter(j, extra_bits)

    def others(fn, mine=slot, count=n):
        def step(off, carry):
            fn(lax.rem(mine + off, count))
            return carry

        lax.fori_loop(1, count, step, 0)

    quarter = n // 4
    column = lax.div(slot, quarter)
    upper = lax.div(column, 2)
    inner = column + upper * (3 - 2 * column)

    def far_first(fn, ranks=(0, 1, 2, 3)):
        for rank in ranks:
            place = (3, 2, 1 - inner, inner)[rank]
            base = (place + upper * (3 - 2 * place)) * quarter

            def step(k, carry):
                fn(base + lax.rem(slot + 1 + k, quarter))
                return carry

            for k in range(quarter - (rank == 3)):
                step(k, 0)

    def owners_far_first(fn, among=False):
        for rank in range(2):
            base = (2 - rank + upper * (2 * rank - 1)) * quarter

            def step(k, carry):
                fn(base + lax.rem(slot + 1 + k, quarter))
                return carry

            for k in range(quarter - rank):
                step(k, 0)

            if rank == 1 and not among:

                @pl.when(jnp.logical_not(is_owner))
                def _():
                    fn(base + lax.rem(slot, quarter))

    is_owner = inner == 1

    def remote(src, dst, phase, target):
        return pltpu.make_async_remote_copy(
            src_ref=src,
            dst_ref=dst,
            send_sem=send_sem.at[phase],
            recv_sem=recv_sem.at[phase],
            device_id={"groups": group, "long": target},
            device_id_type=MESH,
        )

    def block(ref, j, size):
        return ref.at[:, pl.ds(pl.multiple_of(j * size, size), size), :]

    def arrived(ref, phase):
        remote(ref, ref, phase, peer(lax.rem(slot + 1, n))).wait_recv()

    def departed(ref, phase):
        remote(ref, ref, phase, peer(lax.rem(slot + 1, n))).wait_send()

    index = slot - first

    def shard(k):
        return lax.rem(k, 2) * (owners // 2) + lax.div(k, 2)

    def signal(j, target):
        pl.semaphore_signal(
            barrier, inc=1, device_id={"groups": group, "long": target(j)}, device_id_type=MESH
        )

    barrier = pltpu.get_barrier_semaphore()

    @pl.when(is_owner)
    def _():
        far_first(lambda j: signal(j, peer))
        if extra > 1:
            others(lambda j: signal(j, layer_peer), layer, extra)
        pl.semaphore_wait(barrier, owners + extra - 2)

    @pl.when(jnp.logical_not(is_owner))
    def _():
        pl.semaphore_wait(barrier, owners)

    def inward(src, dst, phase):
        return lambda j: remote(block(src, j - first, per), block(dst, slot, per), phase, peer(j)).start()

    def outward(src, dst, phase):
        return lambda j: remote(block(src, j, per), block(dst, index, per), phase, peer(j)).start()

    def bit_of(q):
        return lax.rem(lax.div(slot, 2**q), 2)

    def flipped(q):
        return peer(slot + (1 - 2 * bit_of(q)) * 2**q)

    def variant(near, far):
        return near + 2 * far

    near_bit, far_bit = bit_of(order[2]), bit_of(order[3])
    mine_at = variant(near_bit, far_bit)
    other_at = variant(near_bit, 1 - far_bit)
    chunks = owners // 2
    chips = owners // 2
    wide = gate // 2
    pair = rows // chunks

    def target_variant(j):
        return variant(lax.rem(lax.div(j, 2 ** order[2]), 2), lax.rem(lax.div(j, 2 ** order[3]), 2))

    def to_final(src, at, j):
        there = j + (far_bit - lax.rem(lax.div(j, 2 ** order[3]), 2)) * 2 ** order[3]
        remote(src(j), block(final.at[target_variant(j)], at, per), FINAL + at, peer(there)).start()

    def to_final_chip(src, at):
        for far in range(2):
            j = slot + (far - far_bit) * 2 ** order[3]
            pltpu.make_async_copy(
                src(j),
                block(final.at[variant(near_bit, far)], at, per),
                recv_sem.at[FINAL + at],
            ).start()
            to_final(src, at, j + (1 - 2 * near_bit) * 2 ** order[2])

    def to_final_side(src, at):
        far_first(lambda j: to_final(src, at, j), (2,))
        to_final_chip(src, at)

    def over_slices(fn, side_far):
        def step(k, carry):
            half = lax.rem(lax.div(k, 2) + upper, 2)
            fn(2 * half + lax.rem(k, 2), 4 * half + 2 * side_far + lax.rem(k, 2))
            return carry

        lax.fori_loop(0, chunks, step, 0)

    def slices(k):
        return [block(final.at[variant(near_bit, far)], k, per) for far in range(2)]

    def two_blocks():
        return block(final.at[mine_at], 0, pair)

    def pass_across():
        def step(chunk, k):
            arrived(two_blocks(), FINAL + k)
            for ref in slices(k):
                remote(ref, ref, FAR + chunk, flipped(order[3])).start()
            for ref in slices(k):
                remote(ref, ref, NEAR, flipped(order[2])).start()

        over_slices(step, far_bit)

    def gather_final():
        def step(chunk, k):
            arrived(two_blocks(), FAR + chunk)
            for ref in slices(k):
                remote(ref, ref, NEAR, flipped(order[2])).start()

        over_slices(step, 1 - far_bit)
        arrived(final.at[pl.ds(0, 2)], NEAR)

    def keep_half(k, bit, x):
        half = gate // 2
        half_gate[k] = jnp.where(bit == 0, x[:half], x[half:])

    def fit(s):
        return polar(jnp.concatenate([ag_buf[s, 0], ag_buf[s, 1]], axis=1), NS_ITERS)

    def half_apply(x, k):
        full = embed_out(half_gate[k, :, :gate], half_gate[k, :, gate:])
        return dot3(split(x), split(full), ((1,), (1,)))

    def before_last():
        outs = []
        for far in range(2):
            both = [joined(final.at[variant(near, far)]) for near in range(2)]
            outs.append(half_apply(swap_rows(jnp.concatenate(both, axis=0), rows), 0))
        x = swap_plane(jnp.concatenate(outs, axis=0), 2 * rows)
        return jnp.concatenate([x[: 2 * rows], x[2 * rows :]], axis=1)

    def last(x):
        x = swap_plane(half_apply(x, 1), rows)
        psi_out[0] = x[:rows]
        psi_out[1] = x[rows:]

    def joined(ref):
        return jnp.concatenate([ref[0], ref[1]], axis=1)

    owners_far_first(inward(adj_in, adj_buf, ADJ_IN))
    owners_far_first(inward(psi_in, psi_buf, PSI_IN))

    def twin(k):
        return lax.rem(k + owners // 2, owners)

    side = first + upper * (owners // 2)
    half_held = n * per // 2

    def near_owners(fn):
        for k in range(1, owners // 2 + 1):
            j = side + lax.rem(slot + k, owners // 2)
            if k < owners // 2:
                fn(j)
            else:

                @pl.when(jnp.logical_not(is_owner))
                def _():
                    fn(j)

    near_owners(
        lambda j: remote(
            block(psi_in, twin(j - first), per), block(psi_twin, slot, per), EXTRA, peer(j)
        ).start()
    )

    def put(ref, x, done):
        for q in done[::-1]:
            x = swap(x, q, per)
        ref[0] = x[:, :gate]
        ref[1] = x[:, gate:]

    def advance_adjoint(phi, s):
        full = split(embed_out(gates[s, 0], gates[s, 1]))
        phi = dot3(split(phi), full, ((1,), (1,)))
        if s in CHAINED:
            for u, rows_u in enumerate(halves(phi, order[s], per)):
                high, low = split(rows_u.T)
                phi_cross[CHAINED.index(s), u, 0] = high
                phi_cross[CHAINED.index(s), u, 1] = low
        else:
            high, low = split(phi.T)
            phi_t[s, 0] = high
            phi_t[s, 1] = low
        return phi

    def outer(left, right):
        both = dot3(left, right, ((1,), (0,)))
        return both[:gate, :gate] + both[gate:, gate:], both[gate:, :gate] - both[:gate, gate:]

    def own_copy(src, dst, phase):
        return pltpu.make_async_copy(src, dst, recv_sem.at[phase])

    @pl.when(is_owner)
    def _():
        gate_copy = pltpu.make_async_copy(gates_in, gates, local_sem.at[0])
        gate_copy.start()
        own_copy(block(adj_in, index, per), block(adj_buf, slot, per), ADJ_IN).start()
        own_copy(block(psi_in, index, per), block(psi_buf, slot, per), PSI_IN).start()
        own_copy(block(psi_in, twin(index), per), block(psi_twin, slot, per), EXTRA).start()
        chip = lax.div(index, 2)
        parity = lax.rem(index, 2)
        mine = pl.ds(pl.multiple_of(shard(index) * own, own), own)

        gate_copy.wait()
        arrived(adj_buf, ADJ_IN)
        phi = joined(adj_buf)
        for s in range(SECTIONS):
            phi = advance_adjoint(swap(phi, order[s], per), s)
        put(adj_send, phi, order)
        own_copy(block(adj_send, slot, per), block(adj_out, index, per), ADJ_OUT).start()
        adj_back = outward(adj_send, adj_out, ADJ_OUT)
        for rank in BACK[SECTIONS]:
            far_first(adj_back, (rank,))
        arrived(psi_buf, PSI_IN)
        psi = swap(joined(psi_buf), order[0], per)
        fitted = None

        def among(fn):
            owners_far_first(fn, True)

        def over_layers(buf, total, kind):
            buf[layer] = total

            def across(j, here):
                return pltpu.make_async_remote_copy(
                    src_ref=buf.at[here],
                    dst_ref=buf.at[here],
                    send_sem=mid_send.at[kind, j],
                    recv_sem=mid_recv.at[kind, here],
                    device_id={"groups": group, "long": layer_peer(j)},
                    device_id_type=MESH,
                )

            others(lambda j: across(j, layer).start(), layer, extra)
            others(lambda j: across(j, j).wait_recv(), layer, extra)
            others(lambda j: across(j, layer).wait_send(), layer, extra)
            total = buf[0]
            for j in range(1, extra):
                total = total + buf[j]
            return total

        def reduced(src, buf, phase):
            arrived(buf.at[pl.ds(0, owners - 1)], phase)
            buf[index] = src[:, mine, :]
            total = buf[0]
            for j in range(1, owners):
                total = total + buf[j]
            return total

        def send_cross(k, u):
            planes = pl.ds(4 * u, 4)
            remote(
                block(cross.at[k, planes], 1 - parity, wide), pair_buf.at[k, planes], CORE + 2 * k + u, flipped(0)
            ).start()

        def pass_cross(k, u):
            planes = pl.ds(4 * u, 4)
            arrived(pair_buf.at[k, planes], CORE + 2 * k + u)
            rows_here = pl.ds(pl.multiple_of(parity * wide, wide), wide)
            chip_buf[k, planes] = cross[k, planes, rows_here, :] + pair_buf[k, planes]

            def step(off, carry):
                there = lax.rem(chip + off, chips)
                remote(
                    block(chip_buf.at[k, planes], there, own),
                    cross_buf.at[k, chip, planes],
                    CROSS + k,
                    peer(first + 2 * there + parity),
                ).start()
                return carry

            lax.fori_loop(1, chips, step, 0)

        def reduced_cross(k):
            arrived(cross_buf.at[k, pl.ds(0, chips - 1)], CROSS + k)
            cross_buf[k, chip] = chip_buf[k, :, pl.ds(pl.multiple_of(chip * own, own), own), :]
            total = cross_buf[k, 0]
            for j in range(1, chips):
                total = total + cross_buf[k, j]
            return total

        def twin_first(u):
            arrived(block(psi_twin, 0, half_held), EXTRA)
            arrived(block(psi_twin, 0, half_held), MIRROR)
            x = swap(apply(swap(joined(psi_twin), order[0], per), u), order[0], per)
            return jnp.where(upper == 0, x[:half_held], x[half_held:])

        def send_twin(x, u):
            x = swap(apply(swap(x, order[1], per), u), order[1], per)
            twin_send[0] = x[:, :gate]
            twin_send[1] = x[:, gate:]
            at = twin(index)

            to_final_side(lambda j: block(twin_send, j - upper * (n // 2), per), at)

        def send_plain(x, done):
            put(psi_send, x, done)
            to_final_side(lambda j: block(psi_send, j, per), index)

        def fill_cross(k, s, x):
            state = split(x)
            for u in range(2):
                for v in range(2):
                    right = tuple(halves(h, order[s + 1], per)[v] for h in state)
                    cross[k, 4 * u + 2 * v], cross[k, 4 * u + 2 * v + 1] = outer(
                        (phi_cross[k, u, 0], phi_cross[k, u, 1]), right
                    )
                send_cross(k, u)
            for u in range(2):
                pass_cross(k, u)

        def apply(x, gate_pair):
            return dot3(split(x), split(embed_out(gate_pair[:, :gate], gate_pair[:, gate:])), ((1,), (1,)))

        outer_peer = 3 * upper * quarter + lax.rem(slot, quarter)

        def share_half(k, bit, x):
            keep_half(k, bit, x)
            if k == 0:
                remote(half_gate.at[k], half_gate.at[k], HALF, peer(outer_peer)).start()

        for s in range(SECTIONS):
            ahead = CHAINED.index(s + 1) if s + 1 in CHAINED else None
            if s in CHAINED:
                k = CHAINED.index(s)
                total = reduced_cross(k)
                if extra > 1:
                    total = over_layers(mid_cross.at[k], total, SECTIONS + k)
                ag_buf[s, 0, mine, :], ag_buf[s, 1, mine, :] = contract_cross(total, fitted)
            else:
                part[s, 0], part[s, 1] = outer((phi_t[s, 0], phi_t[s, 1]), split(psi))
                among(
                    lambda j: remote(block(part.at[s], shard(j - first), own), rs_buf.at[s, index], RS + s, peer(j)).start()
                )
                if ahead is not None:
                    fill_cross(ahead, s, psi)
                if s == 2:
                    send_plain(psi, order[:3])
                total = reduced(part.at[s], rs_buf.at[s], RS + s)
                if extra > 1:
                    total = over_layers(mid_buf.at[s], total, s)
                ag_buf[s, :, mine, :] = total
            held = block(ag_buf.at[s], shard(index), own)
            among(lambda j: remote(held, held, AG + s, peer(j)).start())
            if s == SECTIONS - 1:
                far_first(lambda j: remote(held, held, AG + s, peer(j)).start(), (2, 0))
            if s in CHAINED and s < SECTIONS - 1:
                plain = apply(psi, fitted)
                psi = swap(plain, order[s], per)
                if s == 2:
                    send_plain(plain, order[:2])
                if ahead is not None:
                    fill_cross(ahead, s, psi)
                if s == 2:
                    send_twin(twin_state, fitted)
            for rank in BACK[s]:
                far_first(adj_back, (rank,))
            if s == SECTIONS - 1:
                pass_across()
            arrived(block(ag_buf.at[s], 0, (owners - 1) * own), AG + s)
            if s == 0:
                theirs = block(psi_buf, upper, half_held)
                remote(theirs, block(psi_twin, upper, half_held), MIRROR, peer(first + twin(index))).start()
            if s == 1:
                twin_state = twin_first(fitted)
            fitted = fit(s)
            if s == SECTIONS - 2:
                share_half(0, near_bit, fitted)
            if s == SECTIONS - 1:
                share_half(1, far_bit, fitted)
            if ahead is None and s < SECTIONS - 1:
                psi = swap(apply(psi, fitted), order[s + 1], per)

        gather_final()
        last(before_last())
        for s in range(SECTIONS):
            sent = block(part.at[s], 0, (owners - 1) * own)
            departed(block(psi_send, 0, (n - 1) * own) if s == SECTIONS - 1 else sent, AG + s)
            if s in CHAINED:
                k = CHAINED.index(s)
                departed(block(chip_buf.at[k], 0, (chips - 1) * own), CROSS + k)
                for u in range(2):
                    departed(pair_buf.at[k, pl.ds(4 * u, 4)], CORE + 2 * k + u)
            else:
                departed(sent, RS + s)
        departed(block(adj_in, 0, (owners - 1) * per), ADJ_IN)
        departed(block(psi_in, 0, (owners - 1) * per), PSI_IN)
        departed(block(adj_send, 0, (n - 1) * per), ADJ_OUT)
        departed(block(psi_send, 0, (n // 2 - 2) * per), FINAL + index)
        departed(block(psi_send, 0, (n // 2 - 2) * per), FINAL + twin(index))
        departed(block(psi_in, 0, (owners // 2 - 1) * per), EXTRA)
        departed(block(psi_twin, 0, half_held), MIRROR)
        departed(half_gate.at[0], HALF)

    @pl.when(jnp.logical_not(is_owner))
    def _():
        pass_across()
        gather_final()
        arrived(half_gate.at[0], HALF)
        x = before_last()
        arrived(ag_buf.at[SECTIONS - 1], AG + SECTIONS - 1)
        keep_half(1, far_bit, fit(SECTIONS - 1))
        last(x)
        departed(adj_in, ADJ_IN)
        departed(psi_in, PSI_IN)
        departed(block(psi_in, 0, owners // 2 * per), EXTRA)

    for k in range(chunks):
        departed(block(final.at[mine_at], 0, pair), FAR + k)
    departed(final.at[pl.ds(0, 2)], NEAR)
    arrived(adj_out, ADJ_OUT)


def shards(initial_state, adjoint_state, current_gates):
    bit_count = lax.axis_size("long").bit_length() - 1
    partner_bits = [bit_count - 1, bit_count // 2, 0, 1]
    used = sorted(set(partner_bits))
    assert len(used) == SECTIONS
    order = [used.index(bit) for bit in partner_bits]
    extra_bits = [bit for bit in range(bit_count) if bit not in used]
    n, extra = 2 ** len(used), 2 ** len(extra_bits)
    planes, rows, gate = initial_state.shape
    owners = n // 2
    own = gate // owners
    held = n * (rows // owners)
    f32, bf16 = jnp.float32, jnp.bfloat16
    anywhere = pl.BlockSpec(memory_space=pl.ANY)
    return tuple(
        pl.pallas_call(
            functools.partial(kernel, used, order, extra_bits),
            out_shape=[pltpu.VMEM(initial_state.shape, f32)] * 2,
            in_specs=[anywhere] * 3,
            out_specs=[pl.BlockSpec(memory_space=pltpu.VMEM)] * 2,
            scratch_shapes=[
                pltpu.VMEM((2, held, gate), f32),
                pltpu.VMEM((2, held, gate), f32),
                pltpu.VMEM(current_gates.shape, f32),
                pltpu.VMEM((SECTIONS, 2, 2 * gate, held), bf16),
                pltpu.VMEM((len(CHAINED), 2, 2, 2 * gate, held // 2), bf16),
                pltpu.VMEM((2, held, gate), f32),
                pltpu.VMEM((2, held, gate), f32),
                pltpu.VMEM((2, held, gate), f32),
                pltpu.VMEM((2, held // 2, gate), f32),
                pltpu.VMEM((SECTIONS, 2, gate, gate), f32),
                pltpu.VMEM((SECTIONS, owners, 2, own, gate), f32),
                pltpu.VMEM((len(CHAINED), 8, gate, gate), f32),
                pltpu.VMEM((len(CHAINED), 8, gate // 2, gate), f32),
                pltpu.VMEM((len(CHAINED), 8, gate // 2, gate), f32),
                pltpu.VMEM((len(CHAINED), owners // 2, 8, own, gate), f32),
                pltpu.VMEM((SECTIONS, 2, gate, gate), f32),
                pltpu.VMEM((4, planes, rows, gate), f32),
                pltpu.VMEM((2, gate // 2, 2 * gate), f32),
                pltpu.VMEM((SECTIONS, extra, 2, own, gate), f32),
                pltpu.VMEM((len(CHAINED), extra, 8, own, gate), f32),
                pltpu.SemaphoreType.DMA((PHASES,)),
                pltpu.SemaphoreType.DMA((PHASES,)),
                pltpu.SemaphoreType.DMA((SECTIONS + len(CHAINED) if extra > 1 else 1, extra)),
                pltpu.SemaphoreType.DMA((SECTIONS + len(CHAINED) if extra > 1 else 1, extra)),
                pltpu.SemaphoreType.DMA((1,)),
            ],
            compiler_params=pltpu.CompilerParams(collective_id=0, has_side_effects=True),
            name="sweep",
        )(initial_state, adjoint_state, current_gates)
    )


def solution(mesh):
    return jax.shard_map(
        shards,
        mesh=mesh,
        in_specs=(
            P(None, ("groups", "long"), None),
            P(None, ("groups", "long"), None),
            P("groups", None, None, None),
        ),
        out_specs=(P(None, ("groups", "long"), None), P(None, ("groups", "long"), None)),
        check_vma=False,
    )
```
